32 devices in a mesh: groups: 2 (over y), depth: 4 (over z), tm: 2 (over x), tile: 2 (over core).
Axes of the slice: x: 2, y: 2, z: 4, core: 2. Of those that a mesh axis runs over, the one named last changes fastest.
Arguments:
- volume: bfloat16 [8, 8, 64, 2048], P(('groups', 'tm'), 'depth', 'tile'), parts along dimension 0, may hold values from 0.099609375 to 3
- background: float32 [16, 64, 2048], P(('groups', 'depth'), 'tile'), parts along dimension 0, may hold values from 0.05 to 1
- measured: bfloat16 [8, 64, 2048], P(('groups', 'tm'), 'tile'), parts along dimension 0, may hold values from 0.29882812 to 5
- psf: bfloat16 [8, 9, 16, 17], P('depth'), may hold values from 8.1539154e-05 to 0.0016326904
Outputs:
- new_volume: bfloat16 [8, 8, 64, 2048], P(('groups', 'tm'), 'depth', 'tile'), parts along dimension 0
- new_background: float32 [16, 64, 2048], P(('groups', 'depth'), 'tile'), parts along dimension 0
The draws below stay inside these ranges and needn't reach their ends.
There are 2 independent parts, one for each index of `groups`. The reference program is written for one: setup_inputs(seed, part) draws one part's arguments, and reference() takes and returns one part's arrays. A program takes and returns all parts, laid end to end along the dimension named above; an argument that names none is the same for every part. Nothing has to cross between parts.
All inputs are finite; a program needn't handle non-finite values.
Results may differ from the reference program's by a relative error of at most 0.0018.
Values may be sent and summed in bfloat16 or wider, within the bound.
No kernel may reach another device: no remote copies, remote signals or barrier semaphores. Data moves between devices by JAX's collectives and lax.ppermute only.
A program may use at most 64 MiB of HBM per device.

```python
import math
import jax
import jax.numpy as jnp
from jax import lax

COLS = 2048
PITCH = 16
TAPS = 9
KWIDTH = 17
DEPTHS = 8
FRAMES = 4
ROWS = 64


def block_levels(key, dims, pieces, least, high):
    level, own = 1.0, jax.random.fold_in(key, 6)
    for position, parts in pieces:
        draws = jnp.exp(jax.random.uniform(jax.random.fold_in(own, position), (parts,), jnp.float32, least / len(pieces), high / len(pieces)))
        level = level * jnp.repeat(draws, dims[position] // parts).reshape([-1 if axis == position else 1 for axis in range(len(dims))])
    return level


def setup_inputs(seed: int = 0, part: int = 0) -> dict:
    streams_of = jax.random.split(jax.random.key(seed), 5)
    part_splits = jax.random.split(jax.random.fold_in(streams_of[4], part), 5)
    volume = jnp.clip(jnp.exp(math.log(3.0) - 3.4051113 * jax.random.uniform(part_splits[0], (FRAMES, DEPTHS, ROWS, COLS), jnp.float32) ** block_levels(part_splits[0], (FRAMES, DEPTHS, ROWS, COLS), ((0, 2), (1, 4), (2, 2)), -0.2, 0.2)), 0.099609375, 3.0).astype(jnp.bfloat16)
    background = jnp.clip(jnp.exp(math.log(1.0) - 2.9957323 * jax.random.uniform(part_splits[1], (DEPTHS, ROWS, COLS), jnp.float32) ** block_levels(part_splits[1], (DEPTHS, ROWS, COLS), ((0, 4), (1, 2)), -0.2, 0.2)), 0.05, 1.0)
    measured = jnp.clip(jnp.exp(math.log(5.0) - 2.8173246 * jax.random.uniform(part_splits[2], (FRAMES, ROWS, COLS), jnp.float32) ** block_levels(part_splits[2], (FRAMES, ROWS, COLS), ((0, 2), (1, 2)), -0.2, 0.2)), 0.29882812, 5.0).astype(jnp.bfloat16)
    psf = jnp.clip(jnp.exp(math.log(0.0016326904) - 2.9969012 * jax.random.uniform(streams_of[3], (DEPTHS, TAPS, PITCH, KWIDTH), jnp.float32) ** block_levels(streams_of[3], (DEPTHS, TAPS, PITCH, KWIDTH), ((0, 4),), -0.2, 0.2)), 8.153915405273438e-05, 0.0016326904).astype(jnp.bfloat16)
    return {"volume": volume, "background": background, "measured": measured, "psf": psf}


def shift_cols(values, amount):
    width = values.shape[-1]
    size = abs(amount)
    padded = jnp.pad(values, [(0, 0)] * (values.ndim - 1) + [(size, size)])
    start = size - amount
    return lax.slice_in_dim(padded, start, start + width, axis=values.ndim - 1)


def reference(volume, background, measured, psf):
    tap_count = psf.shape[1]
    half_reach = (tap_count - 1) // 2
    kernel_width = psf.shape[3]
    col_reach = (kernel_width - 1) // 2
    row_count = volume.shape[2]
    col_count = volume.shape[3]
    pitch_cols = psf.shape[2]
    psf_wide = psf.astype(jnp.float32)
    tiled = jnp.tile(psf_wide, (1, 1, col_count // pitch_cols, 1))
    emitters = (volume.astype(jnp.float32) + background[None]).astype(jnp.bfloat16)
    padded = jnp.pad(emitters, ((0, 0), (0, 0), (half_reach, half_reach), (0, 0))).astype(jnp.float32)
    padded = jnp.transpose(padded, (1, 0, 2, 3))

    def depth_step(total, items):
        emit_depth, table_depth = items
        for offset in range(tap_count):
            window = emit_depth[:, offset:offset + row_count]
            for column in range(kernel_width):
                total = total + shift_cols(window * table_depth[offset, :, column], column - col_reach)
        return total, None

    start_total = jnp.zeros((volume.shape[0], row_count, col_count), jnp.float32)
    sensor = lax.scan(depth_step, start_total, (padded, tiled))[0]
    ratio_image = (measured.astype(jnp.float32) / sensor).astype(jnp.bfloat16)
    ratio_pad = jnp.pad(ratio_image, ((0, 0), (half_reach, half_reach), (0, 0))).astype(jnp.float32)

    def depth_back(table_depth):
        total = jnp.zeros((volume.shape[0], row_count, col_count), jnp.float32)
        for offset in range(tap_count):
            start_row = tap_count - 1 - offset
            window = ratio_pad[:, start_row:start_row + row_count]
            for column in range(kernel_width):
                total = total + shift_cols(window, col_reach - column) * table_depth[offset, :, column]
        return total

    backprojected = jnp.transpose(lax.map(depth_back, tiled), (1, 0, 2, 3))
    weight = jnp.tile(jnp.sum(psf_wide, axis=(1, 3)), (1, col_count // pitch_cols))
    new_volume = (volume.astype(jnp.float32) * backprojected / weight[None, :, None, :]).astype(jnp.bfloat16)
    frame_total = jnp.sum(backprojected, axis=0)
    new_background = background * frame_total / (volume.shape[0] * weight[:, None, :])
    return new_volume, new_background
```

```python
import functools

import jax
import jax.numpy as jnp
from jax import lax
from jax.experimental import pallas as pl
from jax.experimental.pallas import tpu as pltpu
from jax.sharding import PartitionSpec as P

LANES = 128
F32 = jnp.float32
BF16 = jnp.bfloat16


def rotated(base_ref, row, pitch):
    base = base_ref[pl.ds(row, pitch), :]
    return jnp.concatenate([base if g == 0 else pltpu.roll(base, pitch * g, 1) for g in range(LANES // pitch)], axis=0)


def fill_base(psf_ref, base_ref):
    depth, taps, pitch, width = psf_ref.shape
    reach = (width - 1) // 2
    base_ref[...] = jnp.zeros_like(base_ref)
    for d in range(depth):
        for t in range(taps):
            base_ref[pl.ds((d * taps + t) * pitch, pitch), pl.ds(0, width)] = psf_ref[d, t].astype(F32)
    for d in range(depth):
        for t in range(taps):
            rows = pl.ds((d * taps + t) * pitch, pitch)
            base_ref[rows, :] = pltpu.roll(base_ref[rows, :], LANES - reach, 1, stride=1, stride_axis=0)


def near_mask(width):
    reach = (width - 1) // 2
    row = lax.broadcasted_iota(jnp.int32, (LANES, LANES), 0)
    col = lax.broadcasted_iota(jnp.int32, (LANES, LANES), 1)
    return jnp.abs(row - col) <= reach


def forward_table_kernel(psf_ref, table_ref, base_ref):
    depth, taps, pitch, width = psf_ref.shape
    fill_base(psf_ref, base_ref)
    near = near_mask(width)
    for d in range(depth):
        for t in range(2 * table_ref.shape[1]):
            lanes = pl.ds((t % 2) * LANES, LANES)
            if t < taps:
                band = rotated(base_ref, (d * taps + t) * pitch, pitch)
                table_ref[d, t // 2, pl.ds(0, LANES), lanes] = jnp.where(near, band, 0.0).astype(BF16)
                table_ref[d, t // 2, pl.ds(LANES, LANES), lanes] = jnp.where(near, 0.0, band).astype(BF16)
            else:
                table_ref[d, t // 2, :, lanes] = jnp.zeros((2 * LANES, LANES), BF16)


def backward_table_kernel(psf_ref, measured_ref, got_ref, table_ref, inverse_ref, chunk_ref, base_ref, rows_ref):
    depth, taps, pitch, width = psf_ref.shape
    frames, row_count, col_count = measured_ref.shape
    blocks = col_count // LANES
    extra = got_ref.shape[1]
    chunk_rows = chunk_ref.shape[1]
    fill_base(psf_ref, base_ref)
    near = near_mask(width)
    for d in range(depth):
        total = jnp.zeros((1, LANES), F32)
        lanes = pl.ds(d * LANES, LANES)
        for t in range(taps):
            band = rotated(base_ref, (d * taps + t) * pitch, pitch).T
            total = total + jnp.sum(band, axis=0, keepdims=True)
            table_ref[t, pl.ds(0, LANES), lanes] = jnp.where(near, band, 0.0).astype(BF16)
            table_ref[t, pl.ds(LANES, LANES), lanes] = jnp.where(near, 0.0, band).astype(BF16)
        inverse_ref[d] = 1.0 / total
    tile = lax.axis_index("tile")
    place = lax.axis_index("depth")
    per_frame = rows_ref.shape[0] // frames
    rows_ref[...] = jnp.ones_like(rows_ref)
    for f in range(frames):
        own = f * per_frame + extra * blocks * tile
        other = f * per_frame + row_count * blocks * (1 - tile)
        for j in range(blocks):
            lanes = pl.ds(j * LANES, LANES)
            values = measured_ref[f, :, lanes].astype(F32)
            rows_ref[pl.ds(own + j, row_count, stride=blocks), :] = values
            values = got_ref[f, :, lanes].astype(F32)
            rows_ref[pl.ds(other + j, extra, stride=blocks), :] = values
        for r in range(chunk_rows):
            start = pl.multiple_of(f * per_frame + (place * chunk_rows + r) * blocks, blocks)
            chunk_ref[f, r] = rows_ref[pl.ds(start, blocks), :]


def with_edges(rows_ref, start, count, blocks, after_mask, before_mask):
    here = rows_ref[pl.ds(start, count), :]
    after = rows_ref[pl.ds(start + 1, count), :]
    before = rows_ref[pl.ds(start - 1, count), :]
    edges = jnp.where(after_mask, after, jnp.where(before_mask, before, 0.0))
    return here.astype(BF16), edges.astype(BF16)


def edge_masks(count, blocks):
    row = lax.rem(lax.broadcasted_iota(jnp.int32, (count, LANES), 0), blocks)
    lane = lax.broadcasted_iota(jnp.int32, (count, LANES), 1)
    after = jnp.logical_and(lane < LANES // 2, row < blocks - 1)
    before = jnp.logical_and(lane >= LANES // 2, row > 0)
    return after, before


PAD = 8


def sensor_kernel(chunks, volume_ref, background_ref, got_ref, table_ref, own_ref, *rest):
    sent_refs = rest[: chunks - 1]
    rows_ref, left_ref, sums_ref, whole_ref = rest[chunks - 1 :]
    frames, depth, row_count, col_count = volume_ref.shape
    blocks = col_count // LANES
    pairs = table_ref.shape[1]
    halo = got_ref.shape[2]
    half = halo // 2
    sensor_rows = row_count + half
    windows = sensor_rows + halo + 1
    span = windows * blocks
    tile = lax.axis_index("tile")
    place = lax.axis_index("depth")
    use_after, use_before = edge_masks(blocks, blocks)
    for f in range(frames):
        for d in range(depth):
            first = PAD + (f * depth + d) * span
            own = first + (half + half * tile) * blocks
            other = first + (row_count + half) * blocks * (1 - tile)
            empty = pl.multiple_of(first + (row_count + halo) * blocks * tile, 8)
            rows_ref[pl.ds(empty, half * blocks), :] = jnp.zeros((half * blocks, LANES), F32)
            rows_ref[pl.ds(first + (windows - 1) * blocks, blocks), :] = jnp.zeros((blocks, LANES), F32)
            for j in range(blocks):
                lanes = pl.ds(j * LANES, LANES)
                total = (volume_ref[f, d, :, lanes].astype(F32) + background_ref[d, :, lanes]).astype(BF16).astype(F32)
                rows_ref[pl.ds(own + j, row_count, stride=blocks), :] = total
                rows_ref[pl.ds(other + j, halo, stride=blocks), :] = got_ref[f, d, :, lanes].astype(F32)
            for r in range(windows):
                start = first + r * blocks
                here, edges = with_edges(rows_ref, start, blocks, blocks, use_after, use_before)
                left_ref[pl.ds(start - PAD, blocks), pl.ds(0, LANES)] = here
                left_ref[pl.ds(start - PAD, blocks), pl.ds(LANES, LANES)] = edges
    size = (sensor_rows + 1) * blocks
    chunk_rows = own_ref.shape[1]
    for f in range(frames):
        total = None
        for d in range(depth):
            for p in range(pairs):
                left = left_ref[pl.ds((f * depth + d) * span + 2 * p * blocks, size), :]
                product = jnp.dot(left, table_ref[d, p], preferred_element_type=F32)
                total = product if total is None else total + product
        sums_ref[...] = total
        count = sensor_rows * blocks
        whole_ref[f, pl.ds(0, count), :] = sums_ref[pl.ds(0, count), pl.ds(0, LANES)] + sums_ref[pl.ds(blocks, count), pl.ds(LANES, LANES)]
        if whole_ref.shape[1] > count:
            whole_ref[f, pl.ds(count, whole_ref.shape[1] - count), :] = jnp.ones((whole_ref.shape[1] - count, LANES), F32)
        for s in range(chunks):
            target = lax.rem(place + s, chunks)
            for r in range(chunk_rows):
                start = pl.multiple_of((target * chunk_rows + r) * blocks, blocks)
                values = whole_ref[f, pl.ds(start, blocks), :]
                if s == 0:
                    own_ref[f, r] = values
                else:
                    sent_refs[s - 1][f, r] = values.astype(BF16)


def spread_ratio(chunks, images, get, rows_ref, left_ref, row_count, half, blocks):
    tile = lax.axis_index("tile")
    place = lax.axis_index("depth")
    use_after, use_before = edge_masks(blocks, blocks)
    windows = row_count + 2 * half
    span = windows * blocks
    sensor_rows = row_count + half
    for f in range(images):
        first = PAD + f * max(windows, chunks * get.rows + half) * blocks
        empty = pl.multiple_of(first + sensor_rows * blocks * tile, 8)
        base = first + half * blocks * (1 - tile)
        for s in range(chunks):
            source = lax.rem(place + chunks - s, chunks)
            chunk_rows = get.rows
            for r in range(chunk_rows):
                start = pl.multiple_of(base + (source * chunk_rows + r) * blocks, 8)
                rows_ref[pl.ds(start, blocks), :] = get(s, f, r)
        rows_ref[pl.ds(empty, half * blocks), :] = jnp.zeros((half * blocks, LANES), F32)
        for r in range(windows):
            here, edges = with_edges(rows_ref, first + r * blocks, blocks, blocks, use_after, use_before)
            left_ref[pl.ds(f * span + r * blocks, blocks), pl.ds(0, LANES)] = here
            left_ref[pl.ds(f * span + r * blocks, blocks), pl.ds(LANES, LANES)] = edges


class Chunk:
    def __init__(self, rows, read):
        self.rows = rows
        self.read = read

    def __call__(self, s, f, r):
        return self.read(s, f, r)


def backproject(f, span, taps, row_count, blocks, left_ref, table_ref):
    total = None
    for t in range(taps):
        left = left_ref[pl.ds(f * span + (taps - 1 - t) * blocks, row_count * blocks), :]
        product = jnp.dot(left, table_ref[t], preferred_element_type=F32)
        total = product if total is None else total + product
    return total


def volume_kernel(chunks, half, *refs):
    ratio_refs = refs[:chunks]
    volume_ref, table_ref, inverse_ref, out_ref, rows_ref, left_ref, sums_ref = refs[chunks:]
    frames, depth, row_count, col_count = volume_ref.shape
    blocks = col_count // LANES
    taps = table_ref.shape[0]
    get = Chunk(ratio_refs[0].shape[1], lambda s, f, r: ratio_refs[s][f, r].astype(F32))
    spread_ratio(chunks, frames, get, rows_ref, left_ref, row_count, half, blocks)
    span = (row_count + 2 * half) * blocks
    for f in range(frames):
        total = backproject(f, span, taps, row_count, blocks, left_ref, table_ref)
        for d in range(depth):
            start = (f * depth + d) * row_count * blocks
            sums_ref[pl.ds(start, row_count * blocks), :] = total[:, d * LANES : (d + 1) * LANES]
            for j in range(blocks):
                lanes = pl.ds(j * LANES, LANES)
                back = sums_ref[pl.ds(start + j, row_count, stride=blocks), :]
                value = volume_ref[f, d, :, lanes].astype(F32) * back * inverse_ref[d]
                out_ref[f, d, :, lanes] = value.astype(BF16)


def background_kernel(chunks, half, scale, summed_ref, got_ref, background_ref, table_ref, inverse_ref, out_ref, rows_ref, left_ref, sums_ref):
    depth, row_count, col_count = background_ref.shape
    blocks = col_count // LANES
    taps = table_ref.shape[0]
    get = Chunk(summed_ref.shape[1], lambda s, f, r: summed_ref[s, r].astype(F32) + got_ref[s, r].astype(F32))
    spread_ratio(chunks, 1, get, rows_ref, left_ref, row_count, half, blocks)
    span = (row_count + 2 * half) * blocks
    total = backproject(0, span, taps, row_count, blocks, left_ref, table_ref)
    for d in range(depth):
        start = d * row_count * blocks
        sums_ref[pl.ds(start, row_count * blocks), :] = total[:, d * LANES : (d + 1) * LANES]
        for j in range(blocks):
            lanes = pl.ds(j * LANES, LANES)
            back = sums_ref[pl.ds(start + j, row_count, stride=blocks), :]
            out_ref[d, :, lanes] = background_ref[d, :, lanes] * back * (inverse_ref[d] * scale)


def whole(count):
    return [pl.BlockSpec(memory_space=pltpu.VMEM)] * count


def call(kernel, args, outs, scratch, flops):
    moved = sum(a.size * a.dtype.itemsize for a in args)
    return pl.pallas_call(
        kernel,
        out_shape=outs,
        in_specs=whole(len(args)),
        out_specs=jax.tree.map(lambda _: pl.BlockSpec(memory_space=pltpu.VMEM), outs),
        scratch_shapes=scratch,
        compiler_params=pltpu.CompilerParams(vmem_limit_bytes=40 * 2**20),
        cost_estimate=pl.CostEstimate(flops=flops, bytes_accessed=moved, transcendentals=0),
    )(*args)


def body(volume, background, measured, psf):
    frames, depth, row_count, col_count = volume.shape
    taps, pitch, width = psf.shape[1:]
    half = (taps - 1) // 2
    blocks = col_count // LANES
    pairs = (taps + 1) // 2
    chunks = lax.axis_size("depth")
    splits = lax.axis_size("tm")
    sensor_rows = row_count + half
    chunk_rows = -(-sensor_rows // chunks)
    shape = jax.ShapeDtypeStruct
    vmem = pltpu.VMEM

    tile = lax.axis_index("tile")
    swap = [(0, 1), (1, 0)]

    def edge(values, width, axis):
        size = values.shape[axis]
        return jnp.where(
            tile == 0,
            lax.slice_in_dim(values, size - width, size, axis=axis),
            lax.slice_in_dim(values, 0, width, axis=axis),
        )

    border = (edge(volume, 2 * half, 2).astype(F32) + edge(background, 2 * half, 1)[None]).astype(BF16)
    border = lax.ppermute(border, "tile", swap)
    measured_border = lax.ppermute(edge(measured, half, 1), "tile", swap)

    base = vmem((depth * taps * pitch, LANES), F32)
    forward = call(
        forward_table_kernel,
        (psf,),
        shape((depth, pairs, 2 * LANES, 2 * LANES), BF16),
        [base],
        2 * 10**8,
    )
    windows = sensor_rows + 2 * half + 1
    padded_rows = chunks * chunk_rows
    chunk = (frames, chunk_rows, blocks, LANES)
    parts = call(
        functools.partial(sensor_kernel, chunks),
        (volume, background, border, forward),
        (shape(chunk, F32),) + (shape(chunk, BF16),) * (chunks - 1),
        [
            vmem((frames * depth * windows * blocks + 2 * PAD, LANES), F32),
            vmem((frames * depth * windows * blocks, 2 * LANES), BF16),
            vmem(((sensor_rows + 1) * blocks, 2 * LANES), F32),
            vmem((frames, padded_rows * blocks, LANES), F32),
        ],
        2 * 10**9,
    )
    sensor = parts[0]
    moved = [
        lax.ppermute(parts[s], "depth", [(i, (i + s) % chunks) for i in range(chunks)])
        for s in range(1, chunks)
    ]
    backward, inverse, measured_chunk = call(
        backward_table_kernel,
        (psf, measured, measured_border),
        (
            shape((taps, 2 * LANES, depth * LANES), BF16),
            shape((depth, 1, LANES), F32),
            shape(chunk, F32),
        ),
        [base, vmem((frames * padded_rows * blocks, LANES), F32)],
        2 * 10**8,
    )
    for part in moved:
        sensor = sensor + part.astype(F32)
    ratio = (measured_chunk / sensor).astype(BF16)
    ratios = [ratio] + [
        lax.ppermute(ratio, "depth", [(i, (i + s) % chunks) for i in range(chunks)])
        for s in range(1, chunks)
    ]
    summed = jnp.stack([jnp.sum(r.astype(F32), axis=0) for r in ratios]).astype(BF16)
    if splits == 2:
        others = lax.ppermute(summed, "tm", swap)
    else:
        total = lax.psum(summed.astype(F32), "tm").astype(BF16)
        summed, others = total, jnp.zeros_like(total)
    window_rows = max(row_count + 2 * half, padded_rows + half) * blocks
    new_volume = call(
        functools.partial(volume_kernel, chunks, half),
        (*ratios, volume, backward, inverse),
        shape(volume.shape, BF16),
        [
            vmem((frames * window_rows + 2 * PAD, LANES), F32),
            vmem((frames * (row_count + 2 * half) * blocks, 2 * LANES), BF16),
            vmem((frames * depth * row_count * blocks, LANES), F32),
        ],
        2 * 10**9,
    )
    new_background = call(
        functools.partial(background_kernel, chunks, half, 1.0 / (frames * splits)),
        (summed, others, background, backward, inverse),
        shape(background.shape, F32),
        [
            vmem((window_rows + 2 * PAD, LANES), F32),
            vmem(((row_count + 2 * half) * blocks, 2 * LANES), BF16),
            vmem((depth * row_count * blocks, LANES), F32),
        ],
        10**9,
    )
    return new_volume, new_background


def solution(mesh):
    placed = (
        P(("groups", "tm"), "depth", "tile", None),
        P(("groups", "depth"), "tile", None),
        P(("groups", "tm"), "tile", None),
        P("depth", None, None, None),
    )
    return jax.shard_map(
        body,
        mesh=mesh,
        in_specs=placed,
        out_specs=(
            P(("groups", "tm"), "depth", "tile", None),
            P(("groups", "depth"), "tile", None),
        ),
        check_vma=False,
    )
```

```python
import functools

import jax
import jax.numpy as jnp
from jax import lax
from jax.experimental import pallas as pl
from jax.experimental.pallas import tpu as pltpu
from jax.sharding import PartitionSpec as P

LANES = 128
F32 = jnp.float32
BF16 = jnp.bfloat16


def rotated(base_ref, row, pitch):
    base = base_ref[pl.ds(row, pitch), :]
    return jnp.concatenate([base if g == 0 else pltpu.roll(base, pitch * g, 1) for g in range(LANES // pitch)], axis=0)


def fill_base(psf_ref, base_ref):
    depth, taps, pitch, width = psf_ref.shape
    reach = (width - 1) // 2
    base_ref[...] = jnp.zeros_like(base_ref)
    for d in range(depth):
        for t in range(taps):
            base_ref[pl.ds((d * taps + t) * pitch, pitch), pl.ds(0, width)] = psf_ref[d, t].astype(F32)
    for d in range(depth):
        for t in range(taps):
            rows = pl.ds((d * taps + t) * pitch, pitch)
            base_ref[rows, :] = pltpu.roll(base_ref[rows, :], LANES - reach, 1, stride=1, stride_axis=0)


def near_mask(width):
    reach = (width - 1) // 2
    row = lax.broadcasted_iota(jnp.int32, (LANES, LANES), 0)
    col = lax.broadcasted_iota(jnp.int32, (LANES, LANES), 1)
    return jnp.abs(row - col) <= reach


def border_kernel(volume_ref, background_ref, measured_ref, psf_ref, border_ref, table_ref, volume_edge, background_edge, sems):
    frames, depth, row_count = volume_ref.shape[:3]
    width = border_ref.shape[2]
    tile = lax.axis_index("tile")

    def copies(start):
        rows = pl.ds(start, width)
        return (
            pltpu.make_async_copy(volume_ref.at[:, :, rows, :], volume_edge, sems.at[0]),
            pltpu.make_async_copy(background_ref.at[:, rows, :], background_edge, sems.at[1]),
            pltpu.make_async_copy(measured_ref.at[:, rows, :], border_ref.at[:, depth], sems.at[2]),
        )

    spread = pltpu.make_async_copy(psf_ref, table_ref, sems.at[3])

    @pl.when(tile == 0)
    def _():
        for copy in copies(row_count - width):
            copy.start()

    @pl.when(tile != 0)
    def _():
        for copy in copies(0):
            copy.start()

    spread.start()
    for copy in copies(0):
        copy.wait()
    for f in range(frames):
        for d in range(depth):
            border_ref[f, d] = (volume_edge[f, d].astype(F32) + background_edge[d]).astype(BF16)
    spread.wait()


def forward_table_kernel(psf_ref, table_ref, base_ref):
    depth, taps, pitch, width = psf_ref.shape
    fill_base(psf_ref, base_ref)
    near = near_mask(width)
    for d in range(depth):
        for t in range(2 * table_ref.shape[1]):
            lanes = pl.ds((t % 2) * LANES, LANES)
            if t < taps:
                band = rotated(base_ref, (d * taps + t) * pitch, pitch)
                table_ref[d, t // 2, pl.ds(0, LANES), lanes] = jnp.where(near, band, 0.0).astype(BF16)
                table_ref[d, t // 2, pl.ds(LANES, LANES), lanes] = jnp.where(near, 0.0, band).astype(BF16)
            else:
                table_ref[d, t // 2, :, lanes] = jnp.zeros((2 * LANES, LANES), BF16)


def backward_table_kernel(psf_ref, measured_ref, got_ref, table_ref, inverse_ref, chunk_ref, base_ref, rows_ref):
    depth, taps, pitch, width = psf_ref.shape
    frames, row_count, col_count = measured_ref.shape
    blocks = col_count // LANES
    extra = (taps - 1) // 2
    got_rows = got_ref.shape[2]
    chunk_rows = chunk_ref.shape[1]
    fill_base(psf_ref, base_ref)
    near = near_mask(width)
    for d in range(depth):
        total = jnp.zeros((1, LANES), F32)
        lanes = pl.ds(d * LANES, LANES)
        for t in range(taps):
            band = rotated(base_ref, (d * taps + t) * pitch, pitch).T
            total = total + jnp.sum(band, axis=0, keepdims=True)
            table_ref[t, pl.ds(0, LANES), lanes] = jnp.where(near, band, 0.0).astype(BF16)
            table_ref[t, pl.ds(LANES, LANES), lanes] = jnp.where(near, 0.0, band).astype(BF16)
        inverse_ref[d] = 1.0 / total
    tile = lax.axis_index("tile")
    place = lax.axis_index("depth")
    per_frame = rows_ref.shape[0] // frames
    rows_ref[...] = jnp.ones_like(rows_ref)
    for f in range(frames):
        start = f * per_frame + extra * blocks
        own = start + extra * blocks * tile
        other = start + (row_count * (1 - tile) - (got_rows - extra) * tile) * blocks
        for j in range(blocks):
            lanes = pl.ds(j * LANES, LANES)
            values = measured_ref[f, :, lanes].astype(F32)
            rows_ref[pl.ds(own + j, row_count, stride=blocks), :] = values
            values = got_ref[f, depth, :, lanes].astype(F32)
            rows_ref[pl.ds(other + j, got_rows, stride=blocks), :] = values
        for r in range(chunk_rows):
            at = pl.multiple_of(start + (place * chunk_rows + r) * blocks, blocks)
            chunk_ref[f, r] = rows_ref[pl.ds(at, blocks), :]


def with_edges(rows_ref, start, count, blocks, after_mask, before_mask):
    here = rows_ref[pl.ds(start, count), :]
    after = rows_ref[pl.ds(start + 1, count), :]
    before = rows_ref[pl.ds(start - 1, count), :]
    edges = jnp.where(after_mask, after, jnp.where(before_mask, before, 0.0))
    return here.astype(BF16), edges.astype(BF16)


def edge_masks(count, blocks):
    row = lax.rem(lax.broadcasted_iota(jnp.int32, (count, LANES), 0), blocks)
    lane = lax.broadcasted_iota(jnp.int32, (count, LANES), 1)
    after = jnp.logical_and(lane < LANES // 2, row < blocks - 1)
    before = jnp.logical_and(lane >= LANES // 2, row > 0)
    return after, before


PAD = 8


def sensor_kernel(chunks, volume_ref, background_ref, got_ref, table_ref, own_ref, *rest):
    sent_refs = rest[: chunks - 1]
    rows_ref, left_ref, sums_ref, whole_ref = rest[chunks - 1 :]
    frames, depth, row_count, col_count = volume_ref.shape
    blocks = col_count // LANES
    pairs = table_ref.shape[1]
    halo = got_ref.shape[2]
    half = halo // 2
    sensor_rows = row_count + half
    windows = sensor_rows + halo + 1
    span = windows * blocks
    tile = lax.axis_index("tile")
    place = lax.axis_index("depth")
    use_after, use_before = edge_masks(blocks, blocks)
    for f in range(frames):
        for d in range(depth):
            first = PAD + (f * depth + d) * span
            own = first + (half + half * tile) * blocks
            other = first + (row_count + half) * blocks * (1 - tile)
            empty = pl.multiple_of(first + (row_count + halo) * blocks * tile, 8)
            rows_ref[pl.ds(empty, half * blocks), :] = jnp.zeros((half * blocks, LANES), F32)
            rows_ref[pl.ds(first + (windows - 1) * blocks, blocks), :] = jnp.zeros((blocks, LANES), F32)
            for j in range(blocks):
                lanes = pl.ds(j * LANES, LANES)
                total = (volume_ref[f, d, :, lanes].astype(F32) + background_ref[d, :, lanes]).astype(BF16).astype(F32)
                rows_ref[pl.ds(own + j, row_count, stride=blocks), :] = total
                rows_ref[pl.ds(other + j, halo, stride=blocks), :] = got_ref[f, d, :, lanes].astype(F32)
            for r in range(windows):
                start = first + r * blocks
                here, edges = with_edges(rows_ref, start, blocks, blocks, use_after, use_before)
                left_ref[pl.ds(start - PAD, blocks), pl.ds(0, LANES)] = here
                left_ref[pl.ds(start - PAD, blocks), pl.ds(LANES, LANES)] = edges
    size = (sensor_rows + 1) * blocks
    chunk_rows = own_ref.shape[1]
    for f in range(frames):
        total = None
        for d in range(depth):
            for p in range(pairs):
                left = left_ref[pl.ds((f * depth + d) * span + 2 * p * blocks, size), :]
                product = jnp.dot(left, table_ref[d, p], preferred_element_type=F32)
                total = product if total is None else total + product
        sums_ref[...] = total
        count = sensor_rows * blocks
        whole_ref[f, pl.ds(0, count), :] = sums_ref[pl.ds(0, count), pl.ds(0, LANES)] + sums_ref[pl.ds(blocks, count), pl.ds(LANES, LANES)]
        if whole_ref.shape[1] > count:
            whole_ref[f, pl.ds(count, whole_ref.shape[1] - count), :] = jnp.ones((whole_ref.shape[1] - count, LANES), F32)
        for s in range(chunks):
            target = lax.rem(place + s, chunks)
            for r in range(chunk_rows):
                start = pl.multiple_of((target * chunk_rows + r) * blocks, blocks)
                values = whole_ref[f, pl.ds(start, blocks), :]
                if s == 0:
                    own_ref[f, r] = values
                else:
                    sent_refs[s - 1][f, r] = values.astype(BF16)


def spread_ratio(chunks, images, get, rows_ref, left_ref, row_count, half, blocks):
    tile = lax.axis_index("tile")
    place = lax.axis_index("depth")
    use_after, use_before = edge_masks(blocks, blocks)
    windows = row_count + 2 * half
    span = windows * blocks
    sensor_rows = row_count + half
    for f in range(images):
        first = PAD + f * max(windows, chunks * get.rows + half) * blocks
        empty = pl.multiple_of(first + sensor_rows * blocks * tile, 8)
        base = first + half * blocks * (1 - tile)
        for s in range(chunks):
            source = lax.rem(place + chunks - s, chunks)
            chunk_rows = get.rows
            for r in range(chunk_rows):
                start = pl.multiple_of(base + (source * chunk_rows + r) * blocks, 8)
                rows_ref[pl.ds(start, blocks), :] = get(s, f, r)
        rows_ref[pl.ds(empty, half * blocks), :] = jnp.zeros((half * blocks, LANES), F32)
        for r in range(windows):
            here, edges = with_edges(rows_ref, first + r * blocks, blocks, blocks, use_after, use_before)
            left_ref[pl.ds(f * span + r * blocks, blocks), pl.ds(0, LANES)] = here
            left_ref[pl.ds(f * span + r * blocks, blocks), pl.ds(LANES, LANES)] = edges


class Chunk:
    def __init__(self, rows, read):
        self.rows = rows
        self.read = read

    def __call__(self, s, f, r):
        return self.read(s, f, r)


def backproject(f, span, taps, row_count, blocks, left_ref, table_ref):
    total = None
    for t in range(taps):
        left = left_ref[pl.ds(f * span + (taps - 1 - t) * blocks, row_count * blocks), :]
        product = jnp.dot(left, table_ref[t], preferred_element_type=F32)
        total = product if total is None else total + product
    return total


def volume_kernel(chunks, half, *refs):
    ratio_refs = refs[:chunks]
    volume_ref, table_ref, inverse_ref, out_ref, rows_ref, left_ref, sums_ref = refs[chunks:]
    frames, depth, row_count, col_count = volume_ref.shape
    blocks = col_count // LANES
    taps = table_ref.shape[0]
    get = Chunk(ratio_refs[0].shape[1], lambda s, f, r: ratio_refs[s][f, r].astype(F32))
    spread_ratio(chunks, frames, get, rows_ref, left_ref, row_count, half, blocks)
    span = (row_count + 2 * half) * blocks
    for f in range(frames):
        total = backproject(f, span, taps, row_count, blocks, left_ref, table_ref)
        for d in range(depth):
            start = (f * depth + d) * row_count * blocks
            sums_ref[pl.ds(start, row_count * blocks), :] = total[:, d * LANES : (d + 1) * LANES]
            for j in range(blocks):
                lanes = pl.ds(j * LANES, LANES)
                back = sums_ref[pl.ds(start + j, row_count, stride=blocks), :]
                value = volume_ref[f, d, :, lanes].astype(F32) * back * inverse_ref[d]
                out_ref[f, d, :, lanes] = value.astype(BF16)


def background_kernel(chunks, half, scale, summed_ref, got_ref, background_ref, table_ref, inverse_ref, out_ref, rows_ref, left_ref, sums_ref):
    depth, row_count, col_count = background_ref.shape
    blocks = col_count // LANES
    taps = table_ref.shape[0]
    get = Chunk(summed_ref.shape[1], lambda s, f, r: summed_ref[s, r].astype(F32) + got_ref[s, r].astype(F32))
    spread_ratio(chunks, 1, get, rows_ref, left_ref, row_count, half, blocks)
    span = (row_count + 2 * half) * blocks
    total = backproject(0, span, taps, row_count, blocks, left_ref, table_ref)
    for d in range(depth):
        start = d * row_count * blocks
        sums_ref[pl.ds(start, row_count * blocks), :] = total[:, d * LANES : (d + 1) * LANES]
        for j in range(blocks):
            lanes = pl.ds(j * LANES, LANES)
            back = sums_ref[pl.ds(start + j, row_count, stride=blocks), :]
            out_ref[d, :, lanes] = background_ref[d, :, lanes] * back * (inverse_ref[d] * scale)


def whole(count):
    return [pl.BlockSpec(memory_space=pltpu.VMEM)] * count


def call(kernel, args, outs, scratch, flops):
    moved = sum(a.size * a.dtype.itemsize for a in args)
    return pl.pallas_call(
        kernel,
        out_shape=outs,
        in_specs=whole(len(args)),
        out_specs=jax.tree.map(lambda _: pl.BlockSpec(memory_space=pltpu.VMEM), outs),
        scratch_shapes=scratch,
        compiler_params=pltpu.CompilerParams(vmem_limit_bytes=40 * 2**20),
        cost_estimate=pl.CostEstimate(flops=flops, bytes_accessed=moved, transcendentals=0),
    )(*args)


def body(volume, background, measured, psf):
    frames, depth, row_count, col_count = volume.shape
    taps, pitch, width = psf.shape[1:]
    half = (taps - 1) // 2
    blocks = col_count // LANES
    pairs = (taps + 1) // 2
    chunks = lax.axis_size("depth")
    splits = lax.axis_size("tm")
    sensor_rows = row_count + half
    chunk_rows = -(-sensor_rows // chunks)
    shape = jax.ShapeDtypeStruct
    vmem = pltpu.VMEM

    swap = [(0, 1), (1, 0)]
    sent, table = pl.pallas_call(
        border_kernel,
        out_shape=(shape((frames, depth + 1, 2 * half, col_count), BF16), shape(psf.shape, BF16)),
        in_specs=[pl.BlockSpec(memory_space=pltpu.HBM)] * 4,
        out_specs=(pl.BlockSpec(memory_space=pltpu.VMEM),) * 2,
        scratch_shapes=[
            vmem((frames, depth, 2 * half, col_count), BF16),
            vmem((depth, 2 * half, col_count), F32),
            pltpu.SemaphoreType.DMA((4,)),
        ],
        compiler_params=pltpu.CompilerParams(vmem_limit_bytes=8 * 2**20),
    )(*[pltpu.with_memory_space_constraint(a, pltpu.HBM) for a in (volume, background, measured, psf)])
    border = lax.ppermute(sent, "tile", swap)

    base = vmem((depth * taps * pitch, LANES), F32)
    forward = call(
        forward_table_kernel,
        (table,),
        shape((depth, pairs, 2 * LANES, 2 * LANES), BF16),
        [base],
        2 * 10**8,
    )
    windows = sensor_rows + 2 * half + 1
    padded_rows = chunks * chunk_rows
    chunk = (frames, chunk_rows, blocks, LANES)
    parts = call(
        functools.partial(sensor_kernel, chunks),
        (volume, background, border, forward),
        (shape(chunk, F32),) + (shape(chunk, BF16),) * (chunks - 1),
        [
            vmem((frames * depth * windows * blocks + 2 * PAD, LANES), F32),
            vmem((frames * depth * windows * blocks, 2 * LANES), BF16),
            vmem(((sensor_rows + 1) * blocks, 2 * LANES), F32),
            vmem((frames, padded_rows * blocks, LANES), F32),
        ],
        2 * 10**9,
    )
    sensor = parts[0]
    moved = [
        lax.ppermute(parts[s], "depth", [(i, (i + s) % chunks) for i in range(chunks)])
        for s in range(1, chunks)
    ]
    backward, inverse, measured_chunk = call(
        backward_table_kernel,
        (table, measured, border),
        (
            shape((taps, 2 * LANES, depth * LANES), BF16),
            shape((depth, 1, LANES), F32),
            shape(chunk, F32),
        ),
        [base, vmem((frames * (half + max(padded_rows, row_count + 2 * half)) * blocks, LANES), F32)],
        2 * 10**8,
    )
    for part in moved:
        sensor = sensor + part.astype(F32)
    ratio = (measured_chunk / sensor).astype(BF16)
    ratios = [ratio] + [
        lax.ppermute(ratio, "depth", [(i, (i + s) % chunks) for i in range(chunks)])
        for s in range(1, chunks)
    ]
    summed = jnp.stack([jnp.sum(r.astype(F32), axis=0) for r in ratios]).astype(BF16)
    if splits == 2:
        others = lax.ppermute(summed, "tm", swap)
    else:
        total = lax.psum(summed.astype(F32), "tm").astype(BF16)
        summed, others = total, jnp.zeros_like(total)
    window_rows = max(row_count + 2 * half, padded_rows + half) * blocks
    new_volume = call(
        functools.partial(volume_kernel, chunks, half),
        (*ratios, volume, backward, inverse),
        shape(volume.shape, BF16),
        [
            vmem((frames * window_rows + 2 * PAD, LANES), F32),
            vmem((frames * (row_count + 2 * half) * blocks, 2 * LANES), BF16),
            vmem((frames * depth * row_count * blocks, LANES), F32),
        ],
        2 * 10**9,
    )
    new_background = call(
        functools.partial(background_kernel, chunks, half, 1.0 / (frames * splits)),
        (summed, others, background, backward, inverse),
        shape(background.shape, F32),
        [
            vmem((window_rows + 2 * PAD, LANES), F32),
            vmem(((row_count + 2 * half) * blocks, 2 * LANES), BF16),
            vmem((depth * row_count * blocks, LANES), F32),
        ],
        10**9,
    )
    return new_volume, new_background


def solution(mesh):
    placed = (
        P(("groups", "tm"), "depth", "tile", None),
        P(("groups", "depth"), "tile", None),
        P(("groups", "tm"), "tile", None),
        P("depth", None, None, None),
    )
    return jax.shard_map(
        body,
        mesh=mesh,
        in_specs=placed,
        out_specs=(
            P(("groups", "tm"), "depth", "tile", None),
            P(("groups", "depth"), "tile", None),
        ),
        check_vma=False,
    )
```

```python
import functools

import jax
import jax.numpy as jnp
from jax import lax
from jax.experimental import pallas as pl
from jax.experimental.pallas import tpu as pltpu
from jax.sharding import PartitionSpec as P

LANES = 128
F32 = jnp.float32
BF16 = jnp.bfloat16


def rotated(base_ref, row, pitch):
    base = base_ref[pl.ds(row, pitch), :]
    return jnp.concatenate([base if g == 0 else pltpu.roll(base, pitch * g, 1) for g in range(LANES // pitch)], axis=0)


def fill_base(psf_ref, base_ref):
    depth, taps, pitch, width = psf_ref.shape
    reach = (width - 1) // 2
    base_ref[...] = jnp.zeros_like(base_ref)
    for d in range(depth):
        for t in range(taps):
            base_ref[pl.ds((d * taps + t) * pitch, pitch), pl.ds(0, width)] = psf_ref[d, t].astype(F32)
    for d in range(depth):
        for t in range(taps):
            rows = pl.ds((d * taps + t) * pitch, pitch)
            base_ref[rows, :] = pltpu.roll(base_ref[rows, :], LANES - reach, 1, stride=1, stride_axis=0)


def near_mask(width):
    reach = (width - 1) // 2
    row = lax.broadcasted_iota(jnp.int32, (LANES, LANES), 0)
    col = lax.broadcasted_iota(jnp.int32, (LANES, LANES), 1)
    return jnp.abs(row - col) <= reach


def border_kernel(volume_ref, background_ref, measured_ref, psf_ref, border_ref, table_ref, volume_edge, background_edge, sems):
    frames, depth, row_count = volume_ref.shape[:3]
    width = border_ref.shape[2]
    tile = lax.axis_index("tile")

    def copies(start):
        rows = pl.ds(start, width)
        return (
            pltpu.make_async_copy(volume_ref.at[:, :, rows, :], volume_edge, sems.at[0]),
            pltpu.make_async_copy(background_ref.at[:, rows, :], background_edge, sems.at[1]),
            pltpu.make_async_copy(measured_ref.at[:, rows, :], border_ref.at[:, depth], sems.at[2]),
        )

    spread = pltpu.make_async_copy(psf_ref, table_ref, sems.at[3])

    @pl.when(tile == 0)
    def _():
        for copy in copies(row_count - width):
            copy.start()

    @pl.when(tile != 0)
    def _():
        for copy in copies(0):
            copy.start()

    spread.start()
    for copy in copies(0):
        copy.wait()
    for f in range(frames):
        for d in range(depth):
            border_ref[f, d] = (volume_edge[f, d].astype(F32) + background_edge[d]).astype(BF16)
    spread.wait()


def forward_table_kernel(psf_ref, volume_ref, background_ref, table_ref, left_ref, base_ref, rows_ref):
    depth, taps, pitch, width = psf_ref.shape
    fill_base(psf_ref, base_ref)
    near = near_mask(width)
    for d in range(depth):
        for t in range(2 * table_ref.shape[1]):
            lanes = pl.ds((t % 2) * LANES, LANES)
            if t < taps:
                band = rotated(base_ref, (d * taps + t) * pitch, pitch)
                table_ref[d, t // 2, pl.ds(0, LANES), lanes] = jnp.where(near, band, 0.0).astype(BF16)
                table_ref[d, t // 2, pl.ds(LANES, LANES), lanes] = jnp.where(near, 0.0, band).astype(BF16)
            else:
                table_ref[d, t // 2, :, lanes] = jnp.zeros((2 * LANES, LANES), BF16)
    frames, depth, row_count, col_count = volume_ref.shape
    blocks = col_count // LANES
    half = (taps - 1) // 2
    tile = lax.axis_index("tile")
    masks = edge_masks(blocks, blocks)
    span = left_ref.shape[0] // (frames * depth)
    for f in range(frames):
        for d in range(depth):
            base = (f * depth + d) * row_count * blocks
            for j in range(blocks):
                lanes = pl.ds(j * LANES, LANES)
                total = (volume_ref[f, d, :, lanes].astype(F32) + background_ref[d, :, lanes]).astype(BF16).astype(F32)
                rows_ref[pl.ds(PAD + base + j, row_count, stride=blocks), :] = total
            own = (f * depth + d) * span + (half + half * tile) * blocks
            empty = pl.multiple_of((f * depth + d) * span + (row_count + 2 * half) * blocks * tile, blocks)
            left_ref[pl.ds(empty, half * blocks), :] = jnp.zeros((half * blocks, 2 * LANES), BF16)
            left_ref[pl.ds((f * depth + d + 1) * span - blocks, blocks), :] = jnp.zeros((blocks, 2 * LANES), BF16)
            for r in range(row_count):
                here, edges = with_edges(rows_ref, PAD + base + r * blocks, blocks, blocks, *masks)
                rows = pl.ds(pl.multiple_of(own + r * blocks, blocks), blocks)
                left_ref[rows, pl.ds(0, LANES)] = here
                left_ref[rows, pl.ds(LANES, LANES)] = edges


def backward_table_kernel(psf_ref, measured_ref, got_ref, table_ref, inverse_ref, chunk_ref, base_ref, rows_ref):
    depth, taps, pitch, width = psf_ref.shape
    frames, row_count, col_count = measured_ref.shape
    blocks = col_count // LANES
    extra = (taps - 1) // 2
    got_rows = got_ref.shape[2]
    chunk_rows = chunk_ref.shape[1]
    fill_base(psf_ref, base_ref)
    near = near_mask(width)
    for d in range(depth):
        total = jnp.zeros((1, LANES), F32)
        lanes = pl.ds(d * LANES, LANES)
        for t in range(taps):
            band = rotated(base_ref, (d * taps + t) * pitch, pitch).T
            total = total + jnp.sum(band, axis=0, keepdims=True)
            table_ref[t, pl.ds(0, LANES), lanes] = jnp.where(near, band, 0.0).astype(BF16)
            table_ref[t, pl.ds(LANES, LANES), lanes] = jnp.where(near, 0.0, band).astype(BF16)
        inverse_ref[d] = 1.0 / total
    tile = lax.axis_index("tile")
    place = lax.axis_index("depth")
    per_frame = rows_ref.shape[0] // frames
    rows_ref[...] = jnp.ones_like(rows_ref)
    for f in range(frames):
        start = f * per_frame + extra * blocks
        own = start + extra * blocks * tile
        other = start + (row_count * (1 - tile) - (got_rows - extra) * tile) * blocks
        for j in range(blocks):
            lanes = pl.ds(j * LANES, LANES)
            values = measured_ref[f, :, lanes].astype(F32)
            rows_ref[pl.ds(own + j, row_count, stride=blocks), :] = values
            values = got_ref[f, depth, :, lanes].astype(F32)
            rows_ref[pl.ds(other + j, got_rows, stride=blocks), :] = values
        for r in range(chunk_rows):
            at = pl.multiple_of(start + (place * chunk_rows + r) * blocks, blocks)
            chunk_ref[f, r] = rows_ref[pl.ds(at, blocks), :]


def with_edges(rows_ref, start, count, blocks, after_mask, before_mask):
    here = rows_ref[pl.ds(start, count), :]
    after = rows_ref[pl.ds(start + 1, count), :]
    before = rows_ref[pl.ds(start - 1, count), :]
    edges = jnp.where(after_mask, after, jnp.where(before_mask, before, 0.0))
    return here.astype(BF16), edges.astype(BF16)


def edge_masks(count, blocks):
    row = lax.rem(lax.broadcasted_iota(jnp.int32, (count, LANES), 0), blocks)
    lane = lax.broadcasted_iota(jnp.int32, (count, LANES), 1)
    after = jnp.logical_and(lane < LANES // 2, row < blocks - 1)
    before = jnp.logical_and(lane >= LANES // 2, row > 0)
    return after, before


PAD = 8


def sensor_kernel(chunks, row_count, half, given_ref, got_ref, table_ref, own_ref, *rest):
    sent_refs = rest[: chunks - 1]
    left_ref, rows_ref, sums_ref, whole_ref = rest[chunks - 1 :]
    frames, layers, halo, col_count = got_ref.shape
    depth = layers - 1
    blocks = col_count // LANES
    pairs = table_ref.shape[1]
    sensor_rows = row_count + half
    span = left_ref.shape[0] // (frames * depth)
    tile = lax.axis_index("tile")
    place = lax.axis_index("depth")
    masks = edge_masks(blocks, blocks)
    for f in range(frames):
        for d in range(depth):
            first = (f * depth + d) * halo * blocks
            other = (f * depth + d) * span + (row_count + half) * blocks * (1 - tile)
            for j in range(blocks):
                lanes = pl.ds(j * LANES, LANES)
                rows_ref[pl.ds(PAD + first + j, halo, stride=blocks), :] = got_ref[f, d, :, lanes].astype(F32)
            for r in range(halo):
                here, edges = with_edges(rows_ref, PAD + first + r * blocks, blocks, blocks, *masks)
                rows = pl.ds(pl.multiple_of(other + r * blocks, blocks), blocks)
                left_ref[rows, pl.ds(0, LANES)] = here
                left_ref[rows, pl.ds(LANES, LANES)] = edges
    size = (sensor_rows + 1) * blocks
    chunk_rows = own_ref.shape[1]
    for f in range(frames):
        total = None
        for d in range(depth):
            for p in range(pairs):
                left = left_ref[pl.ds((f * depth + d) * span + 2 * p * blocks, size), :]
                product = jnp.dot(left, table_ref[d, p], preferred_element_type=F32)
                total = product if total is None else total + product
        sums_ref[...] = total
        count = sensor_rows * blocks
        whole_ref[f, pl.ds(0, count), :] = sums_ref[pl.ds(0, count), pl.ds(0, LANES)] + sums_ref[pl.ds(blocks, count), pl.ds(LANES, LANES)]
        if whole_ref.shape[1] > count:
            whole_ref[f, pl.ds(count, whole_ref.shape[1] - count), :] = jnp.ones((whole_ref.shape[1] - count, LANES), F32)
        for s in range(chunks):
            target = lax.rem(place + s, chunks)
            for r in range(chunk_rows):
                start = pl.multiple_of((target * chunk_rows + r) * blocks, blocks)
                values = whole_ref[f, pl.ds(start, blocks), :]
                if s == 0:
                    own_ref[f, r] = values
                else:
                    sent_refs[s - 1][f, r] = values.astype(BF16)


def spread_ratio(chunks, images, get, rows_ref, left_ref, row_count, half, blocks):
    tile = lax.axis_index("tile")
    place = lax.axis_index("depth")
    use_after, use_before = edge_masks(blocks, blocks)
    windows = row_count + 2 * half
    span = windows * blocks
    sensor_rows = row_count + half
    for f in range(images):
        first = PAD + f * max(windows, chunks * get.rows + half) * blocks
        empty = pl.multiple_of(first + sensor_rows * blocks * tile, 8)
        base = first + half * blocks * (1 - tile)
        for s in range(chunks):
            source = lax.rem(place + chunks - s, chunks)
            chunk_rows = get.rows
            for r in range(chunk_rows):
                start = pl.multiple_of(base + (source * chunk_rows + r) * blocks, 8)
                rows_ref[pl.ds(start, blocks), :] = get(s, f, r)
        rows_ref[pl.ds(empty, half * blocks), :] = jnp.zeros((half * blocks, LANES), F32)
        for r in range(windows):
            here, edges = with_edges(rows_ref, first + r * blocks, blocks, blocks, use_after, use_before)
            left_ref[pl.ds(f * span + r * blocks, blocks), pl.ds(0, LANES)] = here
            left_ref[pl.ds(f * span + r * blocks, blocks), pl.ds(LANES, LANES)] = edges


class Chunk:
    def __init__(self, rows, read):
        self.rows = rows
        self.read = read

    def __call__(self, s, f, r):
        return self.read(s, f, r)


def backproject(f, span, taps, row_count, blocks, left_ref, table_ref):
    total = None
    for t in range(taps):
        left = left_ref[pl.ds(f * span + (taps - 1 - t) * blocks, row_count * blocks), :]
        product = jnp.dot(left, table_ref[t], preferred_element_type=F32)
        total = product if total is None else total + product
    return total


def volume_kernel(chunks, half, *refs):
    ratio_refs = refs[:chunks]
    volume_ref, table_ref, inverse_ref, out_ref, rows_ref, left_ref, sums_ref = refs[chunks:]
    frames, depth, row_count, col_count = volume_ref.shape
    blocks = col_count // LANES
    taps = table_ref.shape[0]
    get = Chunk(ratio_refs[0].shape[1], lambda s, f, r: ratio_refs[s][f, r].astype(F32))
    spread_ratio(chunks, frames, get, rows_ref, left_ref, row_count, half, blocks)
    span = (row_count + 2 * half) * blocks
    for f in range(frames):
        total = backproject(f, span, taps, row_count, blocks, left_ref, table_ref)
        for d in range(depth):
            start = (f * depth + d) * row_count * blocks
            sums_ref[pl.ds(start, row_count * blocks), :] = total[:, d * LANES : (d + 1) * LANES]
            for j in range(blocks):
                lanes = pl.ds(j * LANES, LANES)
                back = sums_ref[pl.ds(start + j, row_count, stride=blocks), :]
                value = volume_ref[f, d, :, lanes].astype(F32) * back * inverse_ref[d]
                out_ref[f, d, :, lanes] = value.astype(BF16)


def background_kernel(chunks, half, scale, summed_ref, got_ref, background_ref, table_ref, inverse_ref, out_ref, rows_ref, left_ref, sums_ref):
    depth, row_count, col_count = background_ref.shape
    blocks = col_count // LANES
    taps = table_ref.shape[0]
    get = Chunk(summed_ref.shape[1], lambda s, f, r: summed_ref[s, r].astype(F32) + got_ref[s, r].astype(F32))
    spread_ratio(chunks, 1, get, rows_ref, left_ref, row_count, half, blocks)
    span = (row_count + 2 * half) * blocks
    total = backproject(0, span, taps, row_count, blocks, left_ref, table_ref)
    for d in range(depth):
        start = d * row_count * blocks
        sums_ref[pl.ds(start, row_count * blocks), :] = total[:, d * LANES : (d + 1) * LANES]
        for j in range(blocks):
            lanes = pl.ds(j * LANES, LANES)
            back = sums_ref[pl.ds(start + j, row_count, stride=blocks), :]
            out_ref[d, :, lanes] = background_ref[d, :, lanes] * back * (inverse_ref[d] * scale)


def whole(count):
    return [pl.BlockSpec(memory_space=pltpu.VMEM)] * count


def call(kernel, args, outs, scratch, flops, aliases={}):
    moved = sum(a.size * a.dtype.itemsize for a in args)
    return pl.pallas_call(
        kernel,
        out_shape=outs,
        in_specs=whole(len(args)),
        out_specs=jax.tree.map(lambda _: pl.BlockSpec(memory_space=pltpu.VMEM), outs),
        scratch_shapes=scratch,
        input_output_aliases=aliases,
        compiler_params=pltpu.CompilerParams(vmem_limit_bytes=40 * 2**20),
        cost_estimate=pl.CostEstimate(flops=flops, bytes_accessed=moved, transcendentals=0),
    )(*args)


def body(volume, background, measured, psf):
    frames, depth, row_count, col_count = volume.shape
    taps, pitch, width = psf.shape[1:]
    half = (taps - 1) // 2
    blocks = col_count // LANES
    pairs = (taps + 1) // 2
    chunks = lax.axis_size("depth")
    splits = lax.axis_size("tm")
    sensor_rows = row_count + half
    chunk_rows = -(-sensor_rows // chunks)
    shape = jax.ShapeDtypeStruct
    vmem = pltpu.VMEM

    swap = [(0, 1), (1, 0)]
    sent, table = pl.pallas_call(
        border_kernel,
        out_shape=(shape((frames, depth + 1, 2 * half, col_count), BF16), shape(psf.shape, BF16)),
        in_specs=[pl.BlockSpec(memory_space=pltpu.HBM)] * 4,
        out_specs=(pl.BlockSpec(memory_space=pltpu.VMEM),) * 2,
        scratch_shapes=[
            vmem((frames, depth, 2 * half, col_count), BF16),
            vmem((depth, 2 * half, col_count), F32),
            pltpu.SemaphoreType.DMA((4,)),
        ],
        compiler_params=pltpu.CompilerParams(vmem_limit_bytes=8 * 2**20),
    )(*[pltpu.with_memory_space_constraint(a, pltpu.HBM) for a in (volume, background, measured, psf)])
    border = lax.ppermute(sent, "tile", swap)

    base = vmem((depth * taps * pitch, LANES), F32)
    windows = sensor_rows + 2 * half + 1
    left_shape = shape((frames * depth * windows * blocks, 2 * LANES), BF16)
    forward, left = call(
        forward_table_kernel,
        (table, volume, background),
        (shape((depth, pairs, 2 * LANES, 2 * LANES), BF16), left_shape),
        [base, vmem((frames * depth * row_count * blocks + 2 * PAD, LANES), F32)],
        2 * 10**8,
    )
    padded_rows = chunks * chunk_rows
    chunk = (frames, chunk_rows, blocks, LANES)
    parts = call(
        functools.partial(sensor_kernel, chunks, row_count, half),
        (left, border, forward),
        (shape(chunk, F32),) + (shape(chunk, BF16),) * (chunks - 1) + (left_shape,),
        [
            vmem((frames * depth * 2 * half * blocks + 2 * PAD, LANES), F32),
            vmem(((sensor_rows + 1) * blocks, 2 * LANES), F32),
            vmem((frames, padded_rows * blocks, LANES), F32),
        ],
        2 * 10**9,
        {0: chunks},
    )
    sensor = parts[0]
    moved = [
        lax.ppermute(parts[s], "depth", [(i, (i + s) % chunks) for i in range(chunks)])
        for s in range(1, chunks)
    ]
    backward, inverse, measured_chunk = call(
        backward_table_kernel,
        (table, measured, border),
        (
            shape((taps, 2 * LANES, depth * LANES), BF16),
            shape((depth, 1, LANES), F32),
            shape(chunk, F32),
        ),
        [base, vmem((frames * (half + max(padded_rows, row_count + 2 * half)) * blocks, LANES), F32)],
        2 * 10**8,
    )
    for part in moved:
        sensor = sensor + part.astype(F32)
    ratio = (measured_chunk / sensor).astype(BF16)
    ratios = [ratio] + [
        lax.ppermute(ratio, "depth", [(i, (i + s) % chunks) for i in range(chunks)])
        for s in range(1, chunks)
    ]
    summed = jnp.stack([jnp.sum(r.astype(F32), axis=0) for r in ratios]).astype(BF16)
    if splits == 2:
        others = lax.ppermute(summed, "tm", swap)
    else:
        total = lax.psum(summed.astype(F32), "tm").astype(BF16)
        summed, others = total, jnp.zeros_like(total)
    window_rows = max(row_count + 2 * half, padded_rows + half) * blocks
    new_volume = call(
        functools.partial(volume_kernel, chunks, half),
        (*ratios, volume, backward, inverse),
        shape(volume.shape, BF16),
        [
            vmem((frames * window_rows + 2 * PAD, LANES), F32),
            vmem((frames * (row_count + 2 * half) * blocks, 2 * LANES), BF16),
            vmem((frames * depth * row_count * blocks, LANES), F32),
        ],
        2 * 10**9,
    )
    new_background = call(
        functools.partial(background_kernel, chunks, half, 1.0 / (frames * splits)),
        (summed, others, background, backward, inverse),
        shape(background.shape, F32),
        [
            vmem((window_rows + 2 * PAD, LANES), F32),
            vmem(((row_count + 2 * half) * blocks, 2 * LANES), BF16),
            vmem((depth * row_count * blocks, LANES), F32),
        ],
        10**9,
    )
    return new_volume, new_background


def solution(mesh):
    placed = (
        P(("groups", "tm"), "depth", "tile", None),
        P(("groups", "depth"), "tile", None),
        P(("groups", "tm"), "tile", None),
        P("depth", None, None, None),
    )
    return jax.shard_map(
        body,
        mesh=mesh,
        in_specs=placed,
        out_specs=(
            P(("groups", "tm"), "depth", "tile", None),
            P(("groups", "depth"), "tile", None),
        ),
        check_vma=False,
    )
```

```python
import functools

import jax
import jax.numpy as jnp
from jax import lax
from jax.experimental import pallas as pl
from jax.experimental.pallas import tpu as pltpu
from jax.sharding import PartitionSpec as P

LANES = 128
F32 = jnp.float32
BF16 = jnp.bfloat16


def rotated(base_ref, row, pitch):
    base = base_ref[pl.ds(row, pitch), :]
    return jnp.concatenate([base if g == 0 else pltpu.roll(base, pitch * g, 1) for g in range(LANES // pitch)], axis=0)


def fill_base(psf_ref, base_ref):
    depth, taps, pitch, width = psf_ref.shape
    reach = (width - 1) // 2
    base_ref[...] = jnp.zeros_like(base_ref)
    for d in range(depth):
        for t in range(taps):
            base_ref[pl.ds((d * taps + t) * pitch, pitch), pl.ds(0, width)] = psf_ref[d, t].astype(F32)
    for d in range(depth):
        for t in range(taps):
            rows = pl.ds((d * taps + t) * pitch, pitch)
            base_ref[rows, :] = pltpu.roll(base_ref[rows, :], LANES - reach, 1, stride=1, stride_axis=0)


def near_mask(width):
    reach = (width - 1) // 2
    row = lax.broadcasted_iota(jnp.int32, (LANES, LANES), 0)
    col = lax.broadcasted_iota(jnp.int32, (LANES, LANES), 1)
    return jnp.abs(row - col) <= reach


def border_kernel(volume_ref, background_ref, psf_ref, border_ref, table_ref, volume_edge, background_edge, sems):
    frames, depth, row_count = volume_ref.shape[:3]
    half = border_ref.shape[2]
    width = volume_edge.shape[2]
    tile = lax.axis_index("tile")

    def copies(start):
        rows = pl.ds(start, width)
        return (
            pltpu.make_async_copy(volume_ref.at[:, :, rows, :], volume_edge, sems.at[0]),
            pltpu.make_async_copy(background_ref.at[:, rows, :], background_edge, sems.at[1]),
        )

    spread = pltpu.make_async_copy(psf_ref, table_ref, sems.at[2])

    @pl.when(tile == 0)
    def _():
        for copy in copies(row_count - width):
            copy.start()

    @pl.when(tile != 0)
    def _():
        for copy in copies(0):
            copy.start()

    spread.start()
    for copy in copies(0):
        copy.wait()
    for f in range(frames):
        for d in range(depth):
            total = volume_edge[f, d].astype(F32) + background_edge[d]
            border_ref[f, d] = jnp.where(tile == 0, total[width - half :], total[:half]).astype(BF16)
    spread.wait()


def forward_table_kernel(psf_ref, volume_ref, background_ref, table_ref, left_ref, base_ref, rows_ref):
    depth, taps, pitch, width = psf_ref.shape
    fill_base(psf_ref, base_ref)
    near = near_mask(width)
    for d in range(depth):
        for t in range(2 * table_ref.shape[1]):
            lanes = pl.ds((t % 2) * LANES, LANES)
            if t < taps:
                band = rotated(base_ref, (d * taps + t) * pitch, pitch)
                table_ref[d, t // 2, pl.ds(0, LANES), lanes] = jnp.where(near, band, 0.0).astype(BF16)
                table_ref[d, t // 2, pl.ds(LANES, LANES), lanes] = jnp.where(near, 0.0, band).astype(BF16)
            else:
                table_ref[d, t // 2, :, lanes] = jnp.zeros((2 * LANES, LANES), BF16)
    frames, depth, row_count, col_count = volume_ref.shape
    blocks = col_count // LANES
    half = (taps - 1) // 2
    tile = lax.axis_index("tile")
    masks = edge_masks(blocks, blocks)
    span = left_ref.shape[0] // (frames * depth)
    for f in range(frames):
        for d in range(depth):
            base = (f * depth + d) * row_count * blocks
            for j in range(blocks):
                lanes = pl.ds(j * LANES, LANES)
                total = (volume_ref[f, d, :, lanes].astype(F32) + background_ref[d, :, lanes]).astype(BF16).astype(F32)
                rows_ref[pl.ds(PAD + base + j, row_count, stride=blocks), :] = total
            own = (f * depth + d) * span + half * blocks
            empty = pl.multiple_of((f * depth + d) * span + (row_count + half) * blocks * tile, blocks)
            left_ref[pl.ds(empty, half * blocks), :] = jnp.zeros((half * blocks, 2 * LANES), BF16)
            left_ref[pl.ds((f * depth + d + 1) * span - blocks, blocks), :] = jnp.zeros((blocks, 2 * LANES), BF16)
            for r in range(row_count):
                here, edges = with_edges(rows_ref, PAD + base + r * blocks, blocks, blocks, *masks)
                rows = pl.ds(own + r * blocks, blocks)
                left_ref[rows, pl.ds(0, LANES)] = here
                left_ref[rows, pl.ds(LANES, LANES)] = edges


def backward_table_kernel(psf_ref, measured_ref, table_ref, inverse_ref, chunk_ref, base_ref, rows_ref):
    depth, taps, pitch, width = psf_ref.shape
    frames, row_count, col_count = measured_ref.shape
    blocks = col_count // LANES
    chunk_rows = chunk_ref.shape[1]
    fill_base(psf_ref, base_ref)
    near = near_mask(width)
    for d in range(depth):
        total = jnp.zeros((1, LANES), F32)
        lanes = pl.ds(d * LANES, LANES)
        for t in range(taps):
            band = rotated(base_ref, (d * taps + t) * pitch, pitch).T
            total = total + jnp.sum(band, axis=0, keepdims=True)
            table_ref[t, pl.ds(0, LANES), lanes] = jnp.where(near, band, 0.0).astype(BF16)
            table_ref[t, pl.ds(LANES, LANES), lanes] = jnp.where(near, 0.0, band).astype(BF16)
        inverse_ref[d] = 1.0 / total
    place = lax.axis_index("depth")
    per_frame = rows_ref.shape[0] // frames
    if per_frame > row_count * blocks:
        rows_ref[...] = jnp.ones_like(rows_ref)
    for f in range(frames):
        start = f * per_frame
        for j in range(blocks):
            lanes = pl.ds(j * LANES, LANES)
            rows_ref[pl.ds(start + j, row_count, stride=blocks), :] = measured_ref[f, :, lanes].astype(F32)
        for r in range(chunk_rows):
            at = pl.multiple_of(start + (place * chunk_rows + r) * blocks, blocks)
            chunk_ref[f, r] = rows_ref[pl.ds(at, blocks), :]


def with_edges(rows_ref, start, count, blocks, after_mask, before_mask):
    here = rows_ref[pl.ds(start, count), :]
    after = rows_ref[pl.ds(start + 1, count), :]
    before = rows_ref[pl.ds(start - 1, count), :]
    edges = jnp.where(after_mask, after, jnp.where(before_mask, before, 0.0))
    return here.astype(BF16), edges.astype(BF16)


def edge_masks(count, blocks):
    row = lax.rem(lax.broadcasted_iota(jnp.int32, (count, LANES), 0), blocks)
    lane = lax.broadcasted_iota(jnp.int32, (count, LANES), 1)
    after = jnp.logical_and(lane < LANES // 2, row < blocks - 1)
    before = jnp.logical_and(lane >= LANES // 2, row > 0)
    return after, before


PAD = 8


def partners(chunks):
    return [0] + sorted(range(1, chunks), key=lambda mask: (mask != chunks - 1, mask))


def sensor_kernel(chunks, row_count, half, given_ref, got_ref, table_ref, own_ref, *rest):
    sent_refs = rest[: chunks - 1]
    left_ref, rows_ref, sums_ref, whole_ref = rest[chunks - 1 :]
    frames, depth, halo, col_count = got_ref.shape
    blocks = col_count // LANES
    pairs = table_ref.shape[1]
    sensor_rows = row_count
    span = left_ref.shape[0] // (frames * depth)
    tile = lax.axis_index("tile")
    place = lax.axis_index("depth")
    masks = edge_masks(blocks, blocks)
    for f in range(frames):
        for d in range(depth):
            first = (f * depth + d) * halo * blocks
            other = (f * depth + d) * span + (row_count + half) * blocks * (1 - tile)
            for j in range(blocks):
                lanes = pl.ds(j * LANES, LANES)
                rows_ref[pl.ds(PAD + first + j, halo, stride=blocks), :] = got_ref[f, d, :, lanes].astype(F32)
            for r in range(halo):
                here, edges = with_edges(rows_ref, PAD + first + r * blocks, blocks, blocks, *masks)
                rows = pl.ds(pl.multiple_of(other + r * blocks, blocks), blocks)
                left_ref[rows, pl.ds(0, LANES)] = here
                left_ref[rows, pl.ds(LANES, LANES)] = edges
    size = (sensor_rows + 1) * blocks
    chunk_rows = own_ref.shape[1]
    for f in range(frames):
        total = None
        for d in range(depth):
            for p in range(pairs):
                left = left_ref[pl.ds((f * depth + d) * span + 2 * p * blocks, size), :]
                product = jnp.dot(left, table_ref[d, p], preferred_element_type=F32)
                total = product if total is None else total + product
        sums_ref[...] = total
        count = sensor_rows * blocks
        whole_ref[f, pl.ds(0, count), :] = sums_ref[pl.ds(0, count), pl.ds(0, LANES)] + sums_ref[pl.ds(blocks, count), pl.ds(LANES, LANES)]
        if whole_ref.shape[1] > count:
            whole_ref[f, pl.ds(count, whole_ref.shape[1] - count), :] = jnp.ones((whole_ref.shape[1] - count, LANES), F32)
        for s in range(chunks):
            target = place if s == 0 else lax.bitwise_xor(place, partners(chunks)[s])
            for r in range(chunk_rows):
                start = pl.multiple_of((target * chunk_rows + r) * blocks, blocks)
                values = whole_ref[f, pl.ds(start, blocks), :]
                if s == 0:
                    own_ref[f, r] = values
                else:
                    sent_refs[s - 1][f, r] = values.astype(BF16)


def spread_ratio(images, row_count, half, blocks, own, border, rows_ref, left_ref):
    tile = lax.axis_index("tile")
    masks = edge_masks(blocks, blocks)
    windows = row_count + 2 * half
    for f in range(images):
        first = PAD + f * windows * blocks
        for r in range(row_count):
            rows_ref[pl.ds(first + (half + r) * blocks, blocks), :] = own(f, r)
        for r in range(half):
            at = first + ((row_count + half) * (1 - tile) + r) * blocks
            rows_ref[pl.ds(pl.multiple_of(at, 8), blocks), :] = border(f, r)
        empty = pl.multiple_of(first + (row_count + half) * blocks * tile, 8)
        rows_ref[pl.ds(empty, half * blocks), :] = jnp.zeros((half * blocks, LANES), F32)
        for r in range(windows):
            here, edges = with_edges(rows_ref, first + r * blocks, blocks, blocks, *masks)
            rows = pl.ds((f * windows + r) * blocks, blocks)
            left_ref[rows, pl.ds(0, LANES)] = here
            left_ref[rows, pl.ds(LANES, LANES)] = edges


def collect_kernel(chunks, row_count, half, *refs):
    ratio_refs = refs[:chunks]
    image_ref, summed_ref, border_ref, border_sum_ref = refs[chunks:]
    frames, chunk_rows = ratio_refs[0].shape[:2]
    tile = lax.axis_index("tile")
    place = lax.axis_index("depth")
    for s, mask in enumerate(partners(chunks)):
        source = lax.bitwise_xor(place, mask) if s else place
        for r in range(chunk_rows):
            total = None
            for f in range(frames):
                values = ratio_refs[s][f, r]
                image_ref[f, source * chunk_rows + r] = values
                values = values.astype(F32)
                total = values if total is None else total + values
            summed_ref[source * chunk_rows + r] = total.astype(BF16)
    edge = (row_count - half) * (1 - tile)
    for r in range(half):
        border_sum_ref[r] = summed_ref[edge + r]
        for f in range(frames):
            border_ref[f, r] = image_ref[f, edge + r]


def backproject(f, span, taps, row_count, blocks, left_ref, table_ref):
    total = None
    for t in range(taps):
        left = left_ref[pl.ds(f * span + (taps - 1 - t) * blocks, row_count * blocks), :]
        product = jnp.dot(left, table_ref[t], preferred_element_type=F32)
        total = product if total is None else total + product
    return total


def volume_kernel(image_ref, border_ref, volume_ref, table_ref, inverse_ref, out_ref, rows_ref, left_ref, sums_ref):
    frames, depth, row_count, col_count = volume_ref.shape
    half = border_ref.shape[1]
    blocks = col_count // LANES
    taps = table_ref.shape[0]
    spread_ratio(
        frames,
        row_count,
        half,
        blocks,
        lambda f, r: image_ref[f, r].astype(F32),
        lambda f, r: border_ref[f, r].astype(F32),
        rows_ref,
        left_ref,
    )
    span = (row_count + 2 * half) * blocks
    for f in range(frames):
        total = backproject(f, span, taps, row_count, blocks, left_ref, table_ref)
        for d in range(depth):
            start = (f * depth + d) * row_count * blocks
            sums_ref[pl.ds(start, row_count * blocks), :] = total[:, d * LANES : (d + 1) * LANES]
            for j in range(blocks):
                lanes = pl.ds(j * LANES, LANES)
                back = sums_ref[pl.ds(start + j, row_count, stride=blocks), :]
                value = volume_ref[f, d, :, lanes].astype(F32) * back * inverse_ref[d]
                out_ref[f, d, :, lanes] = value.astype(BF16)


def background_kernel(scale, summed_ref, got_ref, border_ref, border_got_ref, background_ref, table_ref, inverse_ref, out_ref, rows_ref, left_ref, sums_ref):
    depth, row_count, col_count = background_ref.shape
    half = border_ref.shape[0]
    blocks = col_count // LANES
    taps = table_ref.shape[0]
    spread_ratio(
        1,
        row_count,
        half,
        blocks,
        lambda f, r: summed_ref[r].astype(F32) + got_ref[r].astype(F32),
        lambda f, r: border_ref[r].astype(F32) + border_got_ref[r].astype(F32),
        rows_ref,
        left_ref,
    )
    span = (row_count + 2 * half) * blocks
    total = backproject(0, span, taps, row_count, blocks, left_ref, table_ref)
    for d in range(depth):
        start = d * row_count * blocks
        sums_ref[pl.ds(start, row_count * blocks), :] = total[:, d * LANES : (d + 1) * LANES]
        for j in range(blocks):
            lanes = pl.ds(j * LANES, LANES)
            back = sums_ref[pl.ds(start + j, row_count, stride=blocks), :]
            out_ref[d, :, lanes] = background_ref[d, :, lanes] * back * (inverse_ref[d] * scale)


def whole(count):
    return [pl.BlockSpec(memory_space=pltpu.VMEM)] * count


def call(kernel, args, outs, scratch, flops, aliases={}):
    moved = sum(a.size * a.dtype.itemsize for a in args)
    return pl.pallas_call(
        kernel,
        out_shape=outs,
        in_specs=whole(len(args)),
        out_specs=jax.tree.map(lambda _: pl.BlockSpec(memory_space=pltpu.VMEM), outs),
        scratch_shapes=scratch,
        input_output_aliases=aliases,
        compiler_params=pltpu.CompilerParams(vmem_limit_bytes=40 * 2**20),
        cost_estimate=pl.CostEstimate(flops=flops, bytes_accessed=moved, transcendentals=0),
    )(*args)


def body(volume, background, measured, psf):
    frames, depth, row_count, col_count = volume.shape
    taps, pitch, width = psf.shape[1:]
    half = (taps - 1) // 2
    blocks = col_count // LANES
    pairs = (taps + 1) // 2
    chunks = lax.axis_size("depth")
    splits = lax.axis_size("tm")
    chunk_rows = -(-row_count // chunks)
    padded_rows = chunks * chunk_rows
    windows = row_count + 2 * half
    shape = jax.ShapeDtypeStruct
    vmem = pltpu.VMEM

    swap = [(0, 1), (1, 0)]
    edge_rows = 8 * -(-half // 8)
    sent, table = pl.pallas_call(
        border_kernel,
        out_shape=(shape((frames, depth, half, col_count), BF16), shape(psf.shape, BF16)),
        in_specs=[pl.BlockSpec(memory_space=pltpu.HBM)] * 3,
        out_specs=(pl.BlockSpec(memory_space=pltpu.VMEM),) * 2,
        scratch_shapes=[
            vmem((frames, depth, edge_rows, col_count), BF16),
            vmem((depth, edge_rows, col_count), F32),
            pltpu.SemaphoreType.DMA((3,)),
        ],
        compiler_params=pltpu.CompilerParams(vmem_limit_bytes=8 * 2**20),
    )(*[pltpu.with_memory_space_constraint(a, pltpu.HBM) for a in (volume, background, psf)])
    border = lax.ppermute(sent, "tile", swap)

    base = vmem((depth * taps * pitch, LANES), F32)
    left_shape = shape((frames * depth * (windows + 1) * blocks, 2 * LANES), BF16)
    forward, left = call(
        forward_table_kernel,
        (table, volume, background),
        (shape((depth, pairs, 2 * LANES, 2 * LANES), BF16), left_shape),
        [base, vmem((frames * depth * row_count * blocks + 2 * PAD, LANES), F32)],
        2 * 10**8,
    )
    chunk = (frames, chunk_rows, blocks, LANES)
    parts = call(
        functools.partial(sensor_kernel, chunks, row_count, half),
        (left, border, forward),
        (shape(chunk, F32),) + (shape(chunk, BF16),) * (chunks - 1) + (left_shape,),
        [
            vmem((frames * depth * half * blocks + 2 * PAD, LANES), F32),
            vmem(((row_count + 1) * blocks, 2 * LANES), F32),
            vmem((frames, padded_rows * blocks, LANES), F32),
        ],
        2 * 10**9,
        {0: chunks},
    )
    sensor = parts[0]
    masks = partners(chunks)
    moved = [
        lax.ppermute(parts[s], "depth", [(i, i ^ masks[s]) for i in range(chunks)])
        for s in range(1, chunks)
    ]
    backward, inverse, measured_chunk = call(
        backward_table_kernel,
        (table, measured),
        (
            shape((taps, 2 * LANES, depth * LANES), BF16),
            shape((depth, 1, LANES), F32),
            shape(chunk, F32),
        ),
        [base, vmem((frames * padded_rows * blocks, LANES), F32)],
        2 * 10**8,
    )
    for part in moved:
        sensor = sensor + part.astype(F32)
    ratio = (measured_chunk / sensor).astype(BF16)
    ratios = [ratio] + [
        lax.ppermute(ratio, "depth", [(i, i ^ masks[s]) for i in range(chunks)])
        for s in range(1, chunks)
    ]
    image, summed, edge, edge_sum = call(
        functools.partial(collect_kernel, chunks, row_count, half),
        tuple(ratios),
        (
            shape((frames, padded_rows, blocks, LANES), BF16),
            shape((padded_rows, blocks, LANES), BF16),
            shape((frames, half, blocks, LANES), BF16),
            shape((half, blocks, LANES), BF16),
        ),
        [],
        10**6,
    )
    if splits == 2:
        got = lax.ppermute(summed, "tm", swap)
        other_got = lax.ppermute(edge_sum, ("tm", "tile"), [(i, 3 - i) for i in range(4)])
    edge = lax.ppermute(edge, "tile", swap)
    other = jnp.sum(edge.astype(F32), axis=0)
    if splits == 2:
        other = other.astype(BF16)
    else:
        summed = lax.psum(summed.astype(F32), "tm").astype(BF16)
        other = lax.psum(other.astype(BF16).astype(F32), "tm").astype(BF16)
        got, other_got = jnp.zeros_like(summed), jnp.zeros_like(other)
    new_background = call(
        functools.partial(background_kernel, 1.0 / (frames * splits)),
        (summed, got, other, other_got, background, backward, inverse),
        shape(background.shape, F32),
        [
            vmem((windows * blocks + 2 * PAD, LANES), F32),
            vmem((windows * blocks, 2 * LANES), BF16),
            vmem((depth * row_count * blocks, LANES), F32),
        ],
        10**9,
    )
    new_volume = call(
        volume_kernel,
        (image, edge, volume, backward, inverse),
        shape(volume.shape, BF16),
        [
            vmem((frames * windows * blocks + 2 * PAD, LANES), F32),
            vmem((frames * windows * blocks, 2 * LANES), BF16),
            vmem((frames * depth * row_count * blocks, LANES), F32),
        ],
        2 * 10**9,
    )
    return new_volume, new_background


def solution(mesh):
    placed = (
        P(("groups", "tm"), "depth", "tile", None),
        P(("groups", "depth"), "tile", None),
        P(("groups", "tm"), "tile", None),
        P("depth", None, None, None),
    )
    return jax.shard_map(
        body,
        mesh=mesh,
        in_specs=placed,
        out_specs=(
            P(("groups", "tm"), "depth", "tile", None),
            P(("groups", "depth"), "tile", None),
        ),
        check_vma=False,
    )
```

```python
import functools

import jax
import jax.numpy as jnp
from jax import lax
from jax.experimental import pallas as pl
from jax.experimental.pallas import tpu as pltpu
from jax.sharding import PartitionSpec as P

LANES = 128
F32 = jnp.float32
BF16 = jnp.bfloat16


def rotated(base_ref, row, pitch):
    base = base_ref[pl.ds(row, pitch), :]
    return jnp.concatenate([base if g == 0 else pltpu.roll(base, pitch * g, 1) for g in range(LANES // pitch)], axis=0)


def fill_base(psf_ref, base_ref):
    depth, taps, pitch, width = psf_ref.shape
    reach = (width - 1) // 2
    base_ref[...] = jnp.zeros_like(base_ref)
    for d in range(depth):
        for t in range(taps):
            base_ref[pl.ds((d * taps + t) * pitch, pitch), pl.ds(0, width)] = psf_ref[d, t].astype(F32)
    for d in range(depth):
        for t in range(taps):
            rows = pl.ds((d * taps + t) * pitch, pitch)
            base_ref[rows, :] = pltpu.roll(base_ref[rows, :], LANES - reach, 1, stride=1, stride_axis=0)


def near_mask(width):
    reach = (width - 1) // 2
    row = lax.broadcasted_iota(jnp.int32, (LANES, LANES), 0)
    col = lax.broadcasted_iota(jnp.int32, (LANES, LANES), 1)
    return jnp.abs(row - col) <= reach


def border_kernel(volume_ref, background_ref, psf_ref, border_ref, table_ref, volume_edge, background_edge, sems):
    frames, depth, row_count = volume_ref.shape[:3]
    half = border_ref.shape[2]
    width = volume_edge.shape[2]
    tile = lax.axis_index("tile")

    def copies(start):
        rows = pl.ds(start, width)
        return (
            pltpu.make_async_copy(volume_ref.at[:, :, rows, :], volume_edge, sems.at[0]),
            pltpu.make_async_copy(background_ref.at[:, rows, :], background_edge, sems.at[1]),
        )

    spread = pltpu.make_async_copy(psf_ref, table_ref, sems.at[2])

    @pl.when(tile == 0)
    def _():
        for copy in copies(row_count - width):
            copy.start()

    @pl.when(tile != 0)
    def _():
        for copy in copies(0):
            copy.start()

    spread.start()
    for copy in copies(0):
        copy.wait()
    for f in range(frames):
        for d in range(depth):
            total = volume_edge[f, d].astype(F32) + background_edge[d]
            border_ref[f, d] = jnp.where(tile == 0, total[width - half :], total[:half]).astype(BF16)
    spread.wait()


def forward_table_kernel(psf_ref, volume_ref, background_ref, table_ref, left_ref, base_ref, rows_ref):
    depth, taps, pitch, width = psf_ref.shape
    fill_base(psf_ref, base_ref)
    near = near_mask(width)
    for d in range(depth):
        for t in range(2 * table_ref.shape[1]):
            lanes = pl.ds((t % 2) * LANES, LANES)
            if t < taps:
                band = rotated(base_ref, (d * taps + t) * pitch, pitch)
                table_ref[d, t // 2, pl.ds(0, LANES), lanes] = jnp.where(near, band, 0.0).astype(BF16)
                table_ref[d, t // 2, pl.ds(LANES, LANES), lanes] = jnp.where(near, 0.0, band).astype(BF16)
            else:
                table_ref[d, t // 2, :, lanes] = jnp.zeros((2 * LANES, LANES), BF16)
    frames, depth, row_count, col_count = volume_ref.shape
    blocks = col_count // LANES
    half = (taps - 1) // 2
    tile = lax.axis_index("tile")
    masks = edge_masks(blocks, blocks)
    span = left_ref.shape[0] // (frames * depth)
    for f in range(frames):
        for d in range(depth):
            base = (f * depth + d) * row_count * blocks
            for j in range(blocks):
                lanes = pl.ds(j * LANES, LANES)
                total = (volume_ref[f, d, :, lanes].astype(F32) + background_ref[d, :, lanes]).astype(BF16).astype(F32)
                rows_ref[pl.ds(PAD + base + j, row_count, stride=blocks), :] = total
            own = (f * depth + d) * span + half * blocks
            empty = pl.multiple_of((f * depth + d) * span + (row_count + half) * blocks * tile, blocks)
            left_ref[pl.ds(empty, half * blocks), :] = jnp.zeros((half * blocks, 2 * LANES), BF16)
            left_ref[pl.ds((f * depth + d + 1) * span - blocks, blocks), :] = jnp.zeros((blocks, 2 * LANES), BF16)
            for r in range(row_count):
                here, edges = with_edges(rows_ref, PAD + base + r * blocks, blocks, blocks, *masks)
                rows = pl.ds(own + r * blocks, blocks)
                left_ref[rows, pl.ds(0, LANES)] = here
                left_ref[rows, pl.ds(LANES, LANES)] = edges


def backward_table_kernel(psf_ref, measured_ref, table_ref, inverse_ref, chunk_ref, base_ref, rows_ref):
    depth, taps, pitch, width = psf_ref.shape
    frames, row_count, col_count = measured_ref.shape
    blocks = col_count // LANES
    chunk_rows = chunk_ref.shape[1]
    fill_base(psf_ref, base_ref)
    near = near_mask(width)
    for d in range(depth):
        total = jnp.zeros((1, LANES), F32)
        lanes = pl.ds(d * LANES, LANES)
        for t in range(taps):
            band = rotated(base_ref, (d * taps + t) * pitch, pitch).T
            total = total + jnp.sum(band, axis=0, keepdims=True)
            table_ref[t, pl.ds(0, LANES), lanes] = jnp.where(near, band, 0.0).astype(BF16)
            table_ref[t, pl.ds(LANES, LANES), lanes] = jnp.where(near, 0.0, band).astype(BF16)
        inverse_ref[d] = 1.0 / total
    place = lax.axis_index("depth")
    per_frame = rows_ref.shape[0] // frames
    if per_frame > row_count * blocks:
        rows_ref[...] = jnp.ones_like(rows_ref)
    for f in range(frames):
        start = f * per_frame
        for j in range(blocks):
            lanes = pl.ds(j * LANES, LANES)
            rows_ref[pl.ds(start + j, row_count, stride=blocks), :] = measured_ref[f, :, lanes].astype(F32)
        for r in range(chunk_rows):
            at = pl.multiple_of(start + (place * chunk_rows + r) * blocks, blocks)
            chunk_ref[f, r] = rows_ref[pl.ds(at, blocks), :]


def with_edges(rows_ref, start, count, blocks, after_mask, before_mask):
    here = rows_ref[pl.ds(start, count), :]
    after = rows_ref[pl.ds(start + 1, count), :]
    before = rows_ref[pl.ds(start - 1, count), :]
    edges = jnp.where(after_mask, after, jnp.where(before_mask, before, 0.0))
    return here.astype(BF16), edges.astype(BF16)


def edge_masks(count, blocks):
    row = lax.rem(lax.broadcasted_iota(jnp.int32, (count, LANES), 0), blocks)
    lane = lax.broadcasted_iota(jnp.int32, (count, LANES), 1)
    after = jnp.logical_and(lane < LANES // 2, row < blocks - 1)
    before = jnp.logical_and(lane >= LANES // 2, row > 0)
    return after, before


PAD = 8


def partners(chunks):
    return [0] + sorted(range(1, chunks), key=lambda mask: (mask != chunks - 1, mask))


def sensor_kernel(chunks, row_count, half, given_ref, got_ref, table_ref, own_ref, *rest):
    sent_refs = rest[: chunks - 1]
    left_ref, rows_ref, sums_ref, whole_ref = rest[chunks - 1 :]
    frames, depth, halo, col_count = got_ref.shape
    blocks = col_count // LANES
    pairs = table_ref.shape[1]
    sensor_rows = row_count
    span = left_ref.shape[0] // (frames * depth)
    tile = lax.axis_index("tile")
    place = lax.axis_index("depth")
    masks = edge_masks(blocks, blocks)
    for f in range(frames):
        for d in range(depth):
            first = (f * depth + d) * halo * blocks
            other = (f * depth + d) * span + (row_count + half) * blocks * (1 - tile)
            for j in range(blocks):
                lanes = pl.ds(j * LANES, LANES)
                rows_ref[pl.ds(PAD + first + j, halo, stride=blocks), :] = got_ref[f, d, :, lanes].astype(F32)
            for r in range(halo):
                here, edges = with_edges(rows_ref, PAD + first + r * blocks, blocks, blocks, *masks)
                rows = pl.ds(pl.multiple_of(other + r * blocks, blocks), blocks)
                left_ref[rows, pl.ds(0, LANES)] = here
                left_ref[rows, pl.ds(LANES, LANES)] = edges
    size = (sensor_rows + 1) * blocks
    chunk_rows = own_ref.shape[1]
    for f in range(frames):
        total = None
        for d in range(depth):
            for p in range(pairs):
                left = left_ref[pl.ds((f * depth + d) * span + 2 * p * blocks, size), :]
                product = jnp.dot(left, table_ref[d, p], preferred_element_type=F32)
                total = product if total is None else total + product
        sums_ref[...] = total
        count = sensor_rows * blocks
        whole_ref[f, pl.ds(0, count), :] = sums_ref[pl.ds(0, count), pl.ds(0, LANES)] + sums_ref[pl.ds(blocks, count), pl.ds(LANES, LANES)]
        if whole_ref.shape[1] > count:
            whole_ref[f, pl.ds(count, whole_ref.shape[1] - count), :] = jnp.ones((whole_ref.shape[1] - count, LANES), F32)
        for s in range(chunks):
            target = place if s == 0 else lax.bitwise_xor(place, partners(chunks)[s])
            for r in range(chunk_rows):
                start = pl.multiple_of((target * chunk_rows + r) * blocks, blocks)
                values = whole_ref[f, pl.ds(start, blocks), :]
                if s == 0:
                    own_ref[f, r] = values
                else:
                    sent_refs[s - 1][f, r] = values.astype(BF16)


def spread_ratio(images, row_count, half, blocks, own, border, rows_ref, left_ref):
    tile = lax.axis_index("tile")
    masks = edge_masks(blocks, blocks)
    windows = row_count + 2 * half
    for f in range(images):
        first = PAD + f * windows * blocks
        for r in range(row_count):
            rows_ref[pl.ds(first + (half + r) * blocks, blocks), :] = own(f, r)
        for r in range(half):
            at = first + ((row_count + half) * (1 - tile) + r) * blocks
            rows_ref[pl.ds(pl.multiple_of(at, 8), blocks), :] = border(f, r)
        empty = pl.multiple_of(first + (row_count + half) * blocks * tile, 8)
        rows_ref[pl.ds(empty, half * blocks), :] = jnp.zeros((half * blocks, LANES), F32)
        for r in range(windows):
            here, edges = with_edges(rows_ref, first + r * blocks, blocks, blocks, *masks)
            rows = pl.ds((f * windows + r) * blocks, blocks)
            left_ref[rows, pl.ds(0, LANES)] = here
            left_ref[rows, pl.ds(LANES, LANES)] = edges


def collect_kernel(chunks, *refs):
    ratio_refs = refs[:chunks]
    image_ref, summed_ref = refs[chunks:]
    frames, chunk_rows = ratio_refs[0].shape[:2]
    place = lax.axis_index("depth")
    for s, mask in enumerate(partners(chunks)):
        source = lax.bitwise_xor(place, mask) if s else place
        for r in range(chunk_rows):
            total = None
            for f in range(frames):
                values = ratio_refs[s][f, r]
                image_ref[f, source * chunk_rows + r] = values
                values = values.astype(F32)
                total = values if total is None else total + values
            summed_ref[source * chunk_rows + r] = total.astype(BF16)


def edge_kernel(row_count, image_ref, summed_ref, border_ref, border_sum_ref):
    frames, half = border_ref.shape[:2]
    edge = (row_count - half) * (1 - lax.axis_index("tile"))
    for r in range(half):
        border_sum_ref[r] = summed_ref[edge + r]
        for f in range(frames):
            border_ref[f, r] = image_ref[f, edge + r]


def backproject(f, span, taps, row_count, blocks, left_ref, table_ref):
    total = None
    for t in range(taps):
        left = left_ref[pl.ds(f * span + (taps - 1 - t) * blocks, row_count * blocks), :]
        product = jnp.dot(left, table_ref[t], preferred_element_type=F32)
        total = product if total is None else total + product
    return total


def volume_kernel(image_ref, border_ref, volume_ref, table_ref, inverse_ref, out_ref, rows_ref, left_ref, sums_ref):
    frames, depth, row_count, col_count = volume_ref.shape
    half = border_ref.shape[1]
    blocks = col_count // LANES
    taps = table_ref.shape[0]
    spread_ratio(
        frames,
        row_count,
        half,
        blocks,
        lambda f, r: image_ref[f, r].astype(F32),
        lambda f, r: border_ref[f, r].astype(F32),
        rows_ref,
        left_ref,
    )
    span = (row_count + 2 * half) * blocks
    for f in range(frames):
        total = backproject(f, span, taps, row_count, blocks, left_ref, table_ref)
        for d in range(depth):
            start = (f * depth + d) * row_count * blocks
            sums_ref[pl.ds(start, row_count * blocks), :] = total[:, d * LANES : (d + 1) * LANES]
            for j in range(blocks):
                lanes = pl.ds(j * LANES, LANES)
                back = sums_ref[pl.ds(start + j, row_count, stride=blocks), :]
                value = volume_ref[f, d, :, lanes].astype(F32) * back * inverse_ref[d]
                out_ref[f, d, :, lanes] = value.astype(BF16)


def background_kernel(scale, summed_ref, got_ref, border_ref, border_got_ref, background_ref, table_ref, inverse_ref, given_ref, out_ref, given_out_ref, rows_ref, left_ref, sums_ref, stage_ref, sems):
    given = pltpu.make_async_copy(given_ref, given_out_ref, sems.at[0])
    given.start()
    depth, row_count, col_count = background_ref.shape
    half = border_ref.shape[0]
    blocks = col_count // LANES
    taps = table_ref.shape[0]
    spread_ratio(
        1,
        row_count,
        half,
        blocks,
        lambda f, r: summed_ref[r].astype(F32) + got_ref[r].astype(F32),
        lambda f, r: border_ref[r].astype(F32) + border_got_ref[r].astype(F32),
        rows_ref,
        left_ref,
    )
    span = (row_count + 2 * half) * blocks
    total = backproject(0, span, taps, row_count, blocks, left_ref, table_ref)
    copies = [given]
    for d in range(depth):
        start = d * row_count * blocks
        sums_ref[pl.ds(start, row_count * blocks), :] = total[:, d * LANES : (d + 1) * LANES]
        for j in range(blocks):
            lanes = pl.ds(j * LANES, LANES)
            back = sums_ref[pl.ds(start + j, row_count, stride=blocks), :]
            stage_ref[d, :, lanes] = background_ref[d, :, lanes] * back * (inverse_ref[d] * scale)
        copies.append(pltpu.make_async_copy(stage_ref.at[d], out_ref.at[d], sems.at[1 + d]))
        copies[-1].start()
    for copy in copies:
        copy.wait()


def whole(count):
    return [pl.BlockSpec(memory_space=pltpu.VMEM)] * count


def call(kernel, args, outs, scratch, flops, aliases={}, place=pltpu.VMEM):
    moved = sum(a.size * a.dtype.itemsize for a in args)
    return pl.pallas_call(
        kernel,
        out_shape=outs,
        in_specs=whole(len(args)),
        out_specs=jax.tree.map(lambda _: pl.BlockSpec(memory_space=place), outs),
        scratch_shapes=scratch,
        input_output_aliases=aliases,
        compiler_params=pltpu.CompilerParams(vmem_limit_bytes=40 * 2**20),
        cost_estimate=pl.CostEstimate(flops=flops, bytes_accessed=min(moved, flops // 100), transcendentals=0),
    )(*args)


def body(volume, background, measured, psf):
    frames, depth, row_count, col_count = volume.shape
    taps, pitch, width = psf.shape[1:]
    half = (taps - 1) // 2
    blocks = col_count // LANES
    pairs = (taps + 1) // 2
    chunks = lax.axis_size("depth")
    splits = lax.axis_size("tm")
    chunk_rows = -(-row_count // chunks)
    padded_rows = chunks * chunk_rows
    windows = row_count + 2 * half
    shape = jax.ShapeDtypeStruct
    vmem = pltpu.VMEM

    swap = [(0, 1), (1, 0)]
    edge_rows = 8 * -(-half // 8)
    sent, table = pl.pallas_call(
        border_kernel,
        out_shape=(shape((frames, depth, half, col_count), BF16), shape(psf.shape, BF16)),
        in_specs=[pl.BlockSpec(memory_space=pltpu.HBM)] * 3,
        out_specs=(pl.BlockSpec(memory_space=pltpu.VMEM),) * 2,
        scratch_shapes=[
            vmem((frames, depth, edge_rows, col_count), BF16),
            vmem((depth, edge_rows, col_count), F32),
            pltpu.SemaphoreType.DMA((3,)),
        ],
        compiler_params=pltpu.CompilerParams(vmem_limit_bytes=8 * 2**20),
    )(*[pltpu.with_memory_space_constraint(a, pltpu.HBM) for a in (volume, background, psf)])
    border = lax.ppermute(sent, "tile", swap)

    base = vmem((depth * taps * pitch, LANES), F32)
    left_shape = shape((frames * depth * (windows + 1) * blocks, 2 * LANES), BF16)
    forward, left = call(
        forward_table_kernel,
        (table, volume, background),
        (shape((depth, pairs, 2 * LANES, 2 * LANES), BF16), left_shape),
        [base, vmem((frames * depth * row_count * blocks + 2 * PAD, LANES), F32)],
        2 * 10**8,
    )
    chunk = (frames, chunk_rows, blocks, LANES)
    parts = call(
        functools.partial(sensor_kernel, chunks, row_count, half),
        (left, border, forward),
        (shape(chunk, F32),) + (shape(chunk, BF16),) * (chunks - 1) + (left_shape,),
        [
            vmem((frames * depth * half * blocks + 2 * PAD, LANES), F32),
            vmem(((row_count + 1) * blocks, 2 * LANES), F32),
            vmem((frames, padded_rows * blocks, LANES), F32),
        ],
        2 * 10**9,
        {0: chunks},
    )
    sensor = parts[0]
    masks = partners(chunks)
    moved = [
        lax.ppermute(parts[s], "depth", [(i, i ^ masks[s]) for i in range(chunks)])
        for s in range(1, chunks)
    ]
    backward, inverse, measured_chunk = call(
        backward_table_kernel,
        (table, measured),
        (
            shape((taps, 2 * LANES, depth * LANES), BF16),
            shape((depth, 1, LANES), F32),
            shape(chunk, F32),
        ),
        [base, vmem((frames * padded_rows * blocks, LANES), F32)],
        2 * 10**8,
    )
    for part in moved:
        sensor = sensor + part.astype(F32)
    ratio = (measured_chunk / sensor).astype(BF16)
    ratios = [ratio] + [
        lax.ppermute(ratio, "depth", [(i, i ^ masks[s]) for i in range(chunks)])
        for s in range(1, chunks)
    ]
    image, summed = call(
        functools.partial(collect_kernel, chunks),
        tuple(ratios),
        (shape((frames, padded_rows, blocks, LANES), BF16), shape((padded_rows, blocks, LANES), BF16)),
        [],
        10**6,
    )
    edge, edge_sum = call(
        functools.partial(edge_kernel, row_count),
        (image, summed),
        (shape((frames, half, blocks, LANES), BF16), shape((half, blocks, LANES), BF16)),
        [],
        1000000000,
    )
    if splits == 2:
        got = lax.ppermute(summed, "tm", swap)
        other_got = lax.ppermute(edge_sum, ("tm", "tile"), [(i, 3 - i) for i in range(4)])
    edge = lax.ppermute(edge, "tile", swap)
    other = jnp.sum(edge.astype(F32), axis=0)
    if splits == 2:
        other = other.astype(BF16)
    else:
        summed = lax.psum(summed.astype(F32), "tm").astype(BF16)
        other = lax.psum(other.astype(BF16).astype(F32), "tm").astype(BF16)
        got, other_got = jnp.zeros_like(summed), jnp.zeros_like(other)
    new_volume = call(
        volume_kernel,
        (image, edge, volume, backward, inverse),
        shape(volume.shape, BF16),
        [
            vmem((frames * windows * blocks + 2 * PAD, LANES), F32),
            vmem((frames * windows * blocks, 2 * LANES), BF16),
            vmem((frames * depth * row_count * blocks, LANES), F32),
        ],
        100000000,
    )
    new_background, new_volume = call(
        functools.partial(background_kernel, 1.0 / (frames * splits)),
        (summed, got, other, other_got, background, backward, inverse, new_volume),
        (shape(background.shape, F32), shape(volume.shape, BF16)),
        [
            vmem((windows * blocks + 2 * PAD, LANES), F32),
            vmem((windows * blocks, 2 * LANES), BF16),
            vmem((depth * row_count * blocks, LANES), F32),
            vmem(background.shape, F32),
            pltpu.SemaphoreType.DMA((1 + depth,)),
        ],
        10**9,
        place=pl.ANY,
    )
    return new_volume, new_background


def solution(mesh):
    placed = (
        P(("groups", "tm"), "depth", "tile", None),
        P(("groups", "depth"), "tile", None),
        P(("groups", "tm"), "tile", None),
        P("depth", None, None, None),
    )
    return jax.shard_map(
        body,
        mesh=mesh,
        in_specs=placed,
        out_specs=(
            P(("groups", "tm"), "depth", "tile", None),
            P(("groups", "depth"), "tile", None),
        ),
        check_vma=False,
    )
```

```python
import functools

import jax
import jax.numpy as jnp
from jax import lax
from jax.experimental import pallas as pl
from jax.experimental.pallas import tpu as pltpu
from jax.sharding import PartitionSpec as P

LANES = 128
F32 = jnp.float32
BF16 = jnp.bfloat16


def rotated(base_ref, row, pitch):
    base = base_ref[pl.ds(row, pitch), :]
    return jnp.concatenate([base if g == 0 else pltpu.roll(base, pitch * g, 1) for g in range(LANES // pitch)], axis=0)


def fill_base(psf_ref, base_ref):
    depth, taps, pitch, width = psf_ref.shape
    reach = (width - 1) // 2
    base_ref[...] = jnp.zeros_like(base_ref)
    for d in range(depth):
        for t in range(taps):
            base_ref[pl.ds((d * taps + t) * pitch, pitch), pl.ds(0, width)] = psf_ref[d, t].astype(F32)
    for d in range(depth):
        for t in range(taps):
            rows = pl.ds((d * taps + t) * pitch, pitch)
            base_ref[rows, :] = pltpu.roll(base_ref[rows, :], LANES - reach, 1, stride=1, stride_axis=0)


def near_mask(width):
    reach = (width - 1) // 2
    row = lax.broadcasted_iota(jnp.int32, (LANES, LANES), 0)
    col = lax.broadcasted_iota(jnp.int32, (LANES, LANES), 1)
    return jnp.abs(row - col) <= reach


def border_kernel(volume_ref, background_ref, psf_ref, border_ref, table_ref, volume_edge, background_edge, sems):
    frames, depth, row_count = volume_ref.shape[:3]
    half = border_ref.shape[2]
    width = volume_edge.shape[2]
    tile = lax.axis_index("tile")

    def copies(start):
        rows = pl.ds(start, width)
        return (
            pltpu.make_async_copy(volume_ref.at[:, :, rows, :], volume_edge, sems.at[0]),
            pltpu.make_async_copy(background_ref.at[:, rows, :], background_edge, sems.at[1]),
        )

    spread = pltpu.make_async_copy(psf_ref, table_ref, sems.at[2])

    @pl.when(tile == 0)
    def _():
        for copy in copies(row_count - width):
            copy.start()

    @pl.when(tile != 0)
    def _():
        for copy in copies(0):
            copy.start()

    spread.start()
    for copy in copies(0):
        copy.wait()
    for f in range(frames):
        for d in range(depth):
            total = volume_edge[f, d].astype(F32) + background_edge[d]
            border_ref[f, d] = jnp.where(tile == 0, total[width - half :], total[:half]).astype(BF16)
    spread.wait()


def forward_table_kernel(psf_ref, volume_ref, background_ref, table_ref, left_ref, edge_ref, base_ref, rows_ref, corner_ref):
    depth, taps, pitch, width = psf_ref.shape
    reach = (width - 1) // 2
    pairs = table_ref.shape[0] - 1
    fill_base(psf_ref, base_ref)
    near = near_mask(width)
    corner_ref[...] = jnp.zeros_like(corner_ref)
    for d in range(depth):
        for t in range(2 * pairs):
            pair, lanes = t // 2, pl.ds((t % 2) * LANES, LANES)
            if t < taps:
                band = rotated(base_ref, (d * taps + t) * pitch, pitch)
                table_ref[pair, pl.ds(d * LANES, LANES), lanes] = jnp.where(near, band, 0.0).astype(BF16)
                far = jnp.where(near, 0.0, band)
                half_row = LANES * (pair // 4)
                shift = d * (LANES // 2) + edge_shift(pair % 4)
                corner_ref[pl.ds(half_row + shift, reach), lanes] = far[:reach]
                corner_ref[pl.ds(half_row + (LANES - reach + shift) % LANES, reach), lanes] = far[LANES - reach :]
            else:
                table_ref[pair, pl.ds(d * LANES, LANES), lanes] = jnp.zeros((LANES, LANES), BF16)
    table_ref[pairs] = corner_ref[...].astype(BF16)
    frames, depth, row_count, col_count = volume_ref.shape
    blocks = col_count // LANES
    half = (taps - 1) // 2
    tile = lax.axis_index("tile")
    masks = edge_masks(blocks, blocks, reach)
    span = left_ref.shape[0] // frames
    for f in range(frames):
        for d in range(depth):
            base = (f * depth + d) * row_count * blocks
            for j in range(blocks):
                lanes = pl.ds(j * LANES, LANES)
                total = (volume_ref[f, d, :, lanes].astype(F32) + background_ref[d, :, lanes]).astype(BF16).astype(F32)
                rows_ref[pl.ds(PAD + base + j, row_count, stride=blocks), :] = total
        own = f * span + half * blocks
        empty = pl.ds(pl.multiple_of(f * span + (row_count + half) * blocks * tile, blocks), half * blocks)
        last = pl.ds((f + 1) * span - blocks, blocks)
        left_ref[empty, :] = jnp.zeros((half * blocks, depth * LANES), BF16)
        edge_ref[empty, :] = jnp.zeros((half * blocks, LANES), F32)
        left_ref[last, :] = jnp.zeros((blocks, depth * LANES), BF16)
        edge_ref[last, :] = jnp.zeros((blocks, LANES), F32)
        for r in range(row_count):
            starts = [PAD + ((f * depth + d) * row_count + r) * blocks for d in range(depth)]
            rows = pl.ds(own + r * blocks, blocks)
            left_ref[rows, :], edge_ref[rows, :] = joined(rows_ref, starts, blocks, masks)


def backward_table_kernel(psf_ref, measured_ref, table_ref, inverse_ref, chunk_ref, base_ref, rows_ref):
    depth, taps, pitch, width = psf_ref.shape
    frames, row_count, col_count = measured_ref.shape
    blocks = col_count // LANES
    chunk_rows = chunk_ref.shape[1]
    fill_base(psf_ref, base_ref)
    near = near_mask(width)
    for d in range(depth):
        total = jnp.zeros((1, LANES), F32)
        lanes = pl.ds(d * LANES, LANES)
        for t in range(taps):
            band = rotated(base_ref, (d * taps + t) * pitch, pitch).T
            total = total + jnp.sum(band, axis=0, keepdims=True)
            table_ref[t, pl.ds(0, LANES), lanes] = jnp.where(near, band, 0.0).astype(BF16)
            table_ref[t, pl.ds(LANES, LANES), lanes] = jnp.where(near, 0.0, band).astype(BF16)
        inverse_ref[d] = 1.0 / total
    place = lax.axis_index("depth")
    per_frame = rows_ref.shape[0] // frames
    if per_frame > row_count * blocks:
        rows_ref[...] = jnp.ones_like(rows_ref)
    for f in range(frames):
        start = f * per_frame
        for j in range(blocks):
            lanes = pl.ds(j * LANES, LANES)
            rows_ref[pl.ds(start + j, row_count, stride=blocks), :] = measured_ref[f, :, lanes].astype(F32)
        for r in range(chunk_rows):
            at = pl.multiple_of(start + (place * chunk_rows + r) * blocks, blocks)
            chunk_ref[f, r] = rows_ref[pl.ds(at, blocks), :]


def with_edges(rows_ref, start, count, blocks, after_mask, before_mask):
    here = rows_ref[pl.ds(start, count), :]
    after = rows_ref[pl.ds(start + 1, count), :]
    before = rows_ref[pl.ds(start - 1, count), :]
    edges = jnp.where(after_mask, after, jnp.where(before_mask, before, 0.0))
    return here.astype(BF16), edges


def edge_masks(count, blocks, reach=LANES // 2):
    row = lax.rem(lax.broadcasted_iota(jnp.int32, (count, LANES), 0), blocks)
    lane = lax.broadcasted_iota(jnp.int32, (count, LANES), 1)
    after = jnp.logical_and(lane < reach, row < blocks - 1)
    before = jnp.logical_and(lane >= LANES - reach, row > 0)
    return after, before


PAD = 8


def partners(chunks):
    return [0] + sorted(range(1, chunks), key=lambda mask: (mask != chunks - 1, mask))


def sensor_kernel(chunks, row_count, half, reach, given_ref, given_edge_ref, got_ref, table_ref, own_ref, *rest):
    sent_refs = rest[: chunks - 1]
    left_ref, edge_ref, rows_ref, packed_ref, sums_ref, whole_ref = rest[chunks - 1 :]
    frames, depth, halo, col_count = got_ref.shape
    blocks = col_count // LANES
    pairs = table_ref.shape[0] - 1
    sensor_rows = row_count
    span = left_ref.shape[0] // frames
    tile = lax.axis_index("tile")
    place = lax.axis_index("depth")
    masks = edge_masks(blocks, blocks, reach)
    for f in range(frames):
        for d in range(depth):
            first = (f * depth + d) * halo * blocks
            for j in range(blocks):
                lanes = pl.ds(j * LANES, LANES)
                rows_ref[pl.ds(PAD + first + j, halo, stride=blocks), :] = got_ref[f, d, :, lanes].astype(F32)
        other = f * span + (row_count + half) * blocks * (1 - tile)
        for r in range(halo):
            starts = [PAD + ((f * depth + d) * halo + r) * blocks for d in range(depth)]
            rows = pl.ds(pl.multiple_of(other + r * blocks, blocks), blocks)
            left_ref[rows, :], edge_ref[rows, :] = joined(rows_ref, starts, blocks, masks)
    size = (sensor_rows + 1) * blocks
    chunk_rows = own_ref.shape[1]
    for f in range(frames):
        for r in range(sensor_rows + 1):
            packed = None
            for pair in range(4):
                values = edge_ref[pl.ds(f * span + (r + 2 * pair) * blocks, blocks), :]
                if pair:
                    values = pltpu.roll(values, edge_shift(pair), 1)
                packed = values if packed is None else packed + values
            rows = pl.ds((f * (sensor_rows + 1) + r) * blocks, blocks)
            packed_ref[rows, pl.ds(0, LANES)] = packed.astype(BF16)
            packed_ref[rows, pl.ds(LANES, LANES)] = edge_ref[pl.ds(f * span + (r + 8) * blocks, blocks), :].astype(BF16)
    for f in range(frames):
        total = None
        for p in range(pairs + 1):
            if p < pairs:
                left = left_ref[pl.ds(f * span + 2 * p * blocks, size), :]
            else:
                left = packed_ref[pl.ds(f * size, size), :]
            product = jnp.dot(left, table_ref[p], preferred_element_type=F32)
            total = product if total is None else total + product
        sums_ref[...] = total
        count = sensor_rows * blocks
        whole_ref[f, pl.ds(0, count), :] = sums_ref[pl.ds(0, count), pl.ds(0, LANES)] + sums_ref[pl.ds(blocks, count), pl.ds(LANES, LANES)]
        if whole_ref.shape[1] > count:
            whole_ref[f, pl.ds(count, whole_ref.shape[1] - count), :] = jnp.ones((whole_ref.shape[1] - count, LANES), F32)
        for s in range(chunks):
            target = place if s == 0 else lax.bitwise_xor(place, partners(chunks)[s])
            for r in range(chunk_rows):
                start = pl.multiple_of((target * chunk_rows + r) * blocks, blocks)
                values = whole_ref[f, pl.ds(start, blocks), :]
                if s == 0:
                    own_ref[f, r] = values
                else:
                    sent_refs[s - 1][f, r] = values.astype(BF16)


def joined(rows_ref, starts, blocks, masks):
    (one, one_edges), (two, two_edges) = [with_edges(rows_ref, start, blocks, blocks, *masks) for start in starts]
    return jnp.concatenate([one, two], axis=1), one_edges + pltpu.roll(two_edges, LANES // 2, 1)


def edge_shift(pair):
    return 32 * (pair % 2) + 16 * (pair // 2)


def spread_ratio(images, row_count, half, blocks, own, border, rows_ref, left_ref):
    tile = lax.axis_index("tile")
    masks = edge_masks(blocks, blocks)
    windows = row_count + 2 * half
    for f in range(images):
        first = PAD + f * windows * blocks
        for r in range(row_count):
            rows_ref[pl.ds(first + (half + r) * blocks, blocks), :] = own(f, r)
        for r in range(half):
            at = first + ((row_count + half) * (1 - tile) + r) * blocks
            rows_ref[pl.ds(pl.multiple_of(at, 8), blocks), :] = border(f, r)
        empty = pl.multiple_of(first + (row_count + half) * blocks * tile, 8)
        rows_ref[pl.ds(empty, half * blocks), :] = jnp.zeros((half * blocks, LANES), F32)
        for r in range(windows):
            here, edges = with_edges(rows_ref, first + r * blocks, blocks, blocks, *masks)
            rows = pl.ds((f * windows + r) * blocks, blocks)
            left_ref[rows, pl.ds(0, LANES)] = here
            left_ref[rows, pl.ds(LANES, LANES)] = edges.astype(BF16)


def collect_kernel(chunks, *refs):
    ratio_refs = refs[:chunks]
    image_ref, summed_ref = refs[chunks:]
    frames, chunk_rows = ratio_refs[0].shape[:2]
    place = lax.axis_index("depth")
    for s, mask in enumerate(partners(chunks)):
        source = lax.bitwise_xor(place, mask) if s else place
        for r in range(chunk_rows):
            total = None
            for f in range(frames):
                values = ratio_refs[s][f, r]
                image_ref[f, source * chunk_rows + r] = values
                values = values.astype(F32)
                total = values if total is None else total + values
            summed_ref[source * chunk_rows + r] = total.astype(BF16)


def edge_kernel(row_count, image_ref, summed_ref, border_ref, border_sum_ref):
    frames, half = border_ref.shape[:2]
    edge = (row_count - half) * (1 - lax.axis_index("tile"))
    for r in range(half):
        border_sum_ref[r] = summed_ref[edge + r]
        for f in range(frames):
            border_ref[f, r] = image_ref[f, edge + r]


def backproject(f, span, taps, row_count, blocks, left_ref, table_ref):
    total = None
    for t in range(taps):
        left = left_ref[pl.ds(f * span + (taps - 1 - t) * blocks, row_count * blocks), :]
        product = jnp.dot(left, table_ref[t], preferred_element_type=F32)
        total = product if total is None else total + product
    return total


def volume_kernel(image_ref, border_ref, volume_ref, table_ref, inverse_ref, out_ref, rows_ref, left_ref, sums_ref):
    frames, depth, row_count, col_count = volume_ref.shape
    half = border_ref.shape[1]
    blocks = col_count // LANES
    taps = table_ref.shape[0]
    spread_ratio(
        frames,
        row_count,
        half,
        blocks,
        lambda f, r: image_ref[f, r].astype(F32),
        lambda f, r: border_ref[f, r].astype(F32),
        rows_ref,
        left_ref,
    )
    span = (row_count + 2 * half) * blocks
    for f in range(frames):
        total = backproject(f, span, taps, row_count, blocks, left_ref, table_ref)
        for d in range(depth):
            start = (f * depth + d) * row_count * blocks
            sums_ref[pl.ds(start, row_count * blocks), :] = total[:, d * LANES : (d + 1) * LANES]
            for j in range(blocks):
                lanes = pl.ds(j * LANES, LANES)
                back = sums_ref[pl.ds(start + j, row_count, stride=blocks), :]
                value = volume_ref[f, d, :, lanes].astype(F32) * back * inverse_ref[d]
                out_ref[f, d, :, lanes] = value.astype(BF16)


def background_kernel(scale, summed_ref, got_ref, border_ref, border_got_ref, background_ref, table_ref, inverse_ref, given_ref, out_ref, given_out_ref, rows_ref, left_ref, sums_ref, stage_ref, sems):
    given = pltpu.make_async_copy(given_ref, given_out_ref, sems.at[0])
    given.start()
    depth, row_count, col_count = background_ref.shape
    half = border_ref.shape[0]
    blocks = col_count // LANES
    taps = table_ref.shape[0]
    spread_ratio(
        1,
        row_count,
        half,
        blocks,
        lambda f, r: summed_ref[r].astype(F32) + got_ref[r].astype(F32),
        lambda f, r: border_ref[r].astype(F32) + border_got_ref[r].astype(F32),
        rows_ref,
        left_ref,
    )
    span = (row_count + 2 * half) * blocks
    total = backproject(0, span, taps, row_count, blocks, left_ref, table_ref)
    copies = [given]
    for d in range(depth):
        start = d * row_count * blocks
        sums_ref[pl.ds(start, row_count * blocks), :] = total[:, d * LANES : (d + 1) * LANES]
        for j in range(blocks):
            lanes = pl.ds(j * LANES, LANES)
            back = sums_ref[pl.ds(start + j, row_count, stride=blocks), :]
            stage_ref[d, :, lanes] = background_ref[d, :, lanes] * back * (inverse_ref[d] * scale)
        copies.append(pltpu.make_async_copy(stage_ref.at[d], out_ref.at[d], sems.at[1 + d]))
        copies[-1].start()
    for copy in copies:
        copy.wait()


def whole(count):
    return [pl.BlockSpec(memory_space=pltpu.VMEM)] * count


def call(kernel, args, outs, scratch, flops, aliases={}, place=pltpu.VMEM):
    moved = sum(a.size * a.dtype.itemsize for a in args)
    return pl.pallas_call(
        kernel,
        out_shape=outs,
        in_specs=whole(len(args)),
        out_specs=jax.tree.map(lambda _: pl.BlockSpec(memory_space=place), outs),
        scratch_shapes=scratch,
        input_output_aliases=aliases,
        compiler_params=pltpu.CompilerParams(vmem_limit_bytes=40 * 2**20),
        cost_estimate=pl.CostEstimate(flops=flops, bytes_accessed=min(moved, flops // 100), transcendentals=0),
    )(*args)


def body(volume, background, measured, psf):
    frames, depth, row_count, col_count = volume.shape
    taps, pitch, width = psf.shape[1:]
    half = (taps - 1) // 2
    reach = (width - 1) // 2
    blocks = col_count // LANES
    pairs = (taps + 1) // 2
    chunks = lax.axis_size("depth")
    splits = lax.axis_size("tm")
    chunk_rows = -(-row_count // chunks)
    padded_rows = chunks * chunk_rows
    windows = row_count + 2 * half
    shape = jax.ShapeDtypeStruct
    vmem = pltpu.VMEM

    swap = [(0, 1), (1, 0)]
    edge_rows = 8 * -(-half // 8)
    sent, table = pl.pallas_call(
        border_kernel,
        out_shape=(shape((frames, depth, half, col_count), BF16), shape(psf.shape, BF16)),
        in_specs=[pl.BlockSpec(memory_space=pltpu.HBM)] * 3,
        out_specs=(pl.BlockSpec(memory_space=pltpu.VMEM),) * 2,
        scratch_shapes=[
            vmem((frames, depth, edge_rows, col_count), BF16),
            vmem((depth, edge_rows, col_count), F32),
            pltpu.SemaphoreType.DMA((3,)),
        ],
        compiler_params=pltpu.CompilerParams(vmem_limit_bytes=8 * 2**20),
    )(*[pltpu.with_memory_space_constraint(a, pltpu.HBM) for a in (volume, background, psf)])
    border = lax.ppermute(sent, "tile", swap)

    base = vmem((depth * taps * pitch, LANES), F32)
    assert depth == 2 and pairs == 5 and 16 * reach == LANES
    left_shape = shape((frames * (windows + 1) * blocks, depth * LANES), BF16)
    edge_shape = shape((frames * (windows + 1) * blocks, LANES), F32)
    forward, left, left_edge = call(
        forward_table_kernel,
        (table, volume, background),
        (shape((pairs + 1, 2 * LANES, 2 * LANES), BF16), left_shape, edge_shape),
        [base, vmem((frames * depth * row_count * blocks + 2 * PAD, LANES), F32), vmem((2 * LANES, 2 * LANES), F32)],
        2 * 10**8,
    )
    chunk = (frames, chunk_rows, blocks, LANES)
    parts = call(
        functools.partial(sensor_kernel, chunks, row_count, half, reach),
        (left, left_edge, border, forward),
        (shape(chunk, F32),) + (shape(chunk, BF16),) * (chunks - 1) + (left_shape, edge_shape),
        [
            vmem((frames * depth * half * blocks + 2 * PAD, LANES), F32),
            vmem((frames * (row_count + 1) * blocks, 2 * LANES), BF16),
            vmem(((row_count + 1) * blocks, 2 * LANES), F32),
            vmem((frames, padded_rows * blocks, LANES), F32),
        ],
        2 * 10**9,
        {0: chunks, 1: chunks + 1},
    )
    sensor = parts[0]
    masks = partners(chunks)
    moved = [
        lax.ppermute(parts[s], "depth", [(i, i ^ masks[s]) for i in range(chunks)])
        for s in range(1, chunks)
    ]
    backward, inverse, measured_chunk = call(
        backward_table_kernel,
        (table, measured),
        (
            shape((taps, 2 * LANES, depth * LANES), BF16),
            shape((depth, 1, LANES), F32),
            shape(chunk, F32),
        ),
        [base, vmem((frames * padded_rows * blocks, LANES), F32)],
        2 * 10**8,
    )
    for part in moved:
        sensor = sensor + part.astype(F32)
    ratio = (measured_chunk / sensor).astype(BF16)
    ratios = [ratio] + [
        lax.ppermute(ratio, "depth", [(i, i ^ masks[s]) for i in range(chunks)])
        for s in range(1, chunks)
    ]
    image, summed = call(
        functools.partial(collect_kernel, chunks),
        tuple(ratios),
        (shape((frames, padded_rows, blocks, LANES), BF16), shape((padded_rows, blocks, LANES), BF16)),
        [],
        10**6,
    )
    edge, edge_sum = call(
        functools.partial(edge_kernel, row_count),
        (image, summed),
        (shape((frames, half, blocks, LANES), BF16), shape((half, blocks, LANES), BF16)),
        [],
        1000000000,
    )
    if splits == 2:
        got = lax.ppermute(summed, "tm", swap)
        other_got = lax.ppermute(edge_sum, ("tm", "tile"), [(i, 3 - i) for i in range(4)])
    edge = lax.ppermute(edge, "tile", swap)
    other = jnp.sum(edge.astype(F32), axis=0)
    if splits == 2:
        other = other.astype(BF16)
    else:
        summed = lax.psum(summed.astype(F32), "tm").astype(BF16)
        other = lax.psum(other.astype(BF16).astype(F32), "tm").astype(BF16)
        got, other_got = jnp.zeros_like(summed), jnp.zeros_like(other)
    new_volume = call(
        volume_kernel,
        (image, edge, volume, backward, inverse),
        shape(volume.shape, BF16),
        [
            vmem((frames * windows * blocks + 2 * PAD, LANES), F32),
            vmem((frames * windows * blocks, 2 * LANES), BF16),
            vmem((frames * depth * row_count * blocks, LANES), F32),
        ],
        100000000,
    )
    new_background, new_volume = call(
        functools.partial(background_kernel, 1.0 / (frames * splits)),
        (summed, got, other, other_got, background, backward, inverse, new_volume),
        (shape(background.shape, F32), shape(volume.shape, BF16)),
        [
            vmem((windows * blocks + 2 * PAD, LANES), F32),
            vmem((windows * blocks, 2 * LANES), BF16),
            vmem((depth * row_count * blocks, LANES), F32),
            vmem(background.shape, F32),
            pltpu.SemaphoreType.DMA((1 + depth,)),
        ],
        10**9,
        place=pl.ANY,
    )
    return new_volume, new_background


def solution(mesh):
    placed = (
        P(("groups", "tm"), "depth", "tile", None),
        P(("groups", "depth"), "tile", None),
        P(("groups", "tm"), "tile", None),
        P("depth", None, None, None),
    )
    return jax.shard_map(
        body,
        mesh=mesh,
        in_specs=placed,
        out_specs=(
            P(("groups", "tm"), "depth", "tile", None),
            P(("groups", "depth"), "tile", None),
        ),
        check_vma=False,
    )
```

```python
import functools

import jax
import jax.numpy as jnp
from jax import lax
from jax.experimental import pallas as pl
from jax.experimental.pallas import tpu as pltpu
from jax.sharding import PartitionSpec as P

LANES = 128
F32 = jnp.float32
BF16 = jnp.bfloat16


def rotated(base_ref, row, pitch):
    base = base_ref[pl.ds(row, pitch), :]
    return jnp.concatenate([base if g == 0 else pltpu.roll(base, pitch * g, 1) for g in range(LANES // pitch)], axis=0)


def fill_base(psf_ref, base_ref):
    depth, taps, pitch, width = psf_ref.shape
    reach = (width - 1) // 2
    base_ref[...] = jnp.zeros_like(base_ref)
    for d in range(depth):
        for t in range(taps):
            base_ref[pl.ds((d * taps + t) * pitch, pitch), pl.ds(0, width)] = psf_ref[d, t].astype(F32)
    for d in range(depth):
        for t in range(taps):
            rows = pl.ds((d * taps + t) * pitch, pitch)
            base_ref[rows, :] = pltpu.roll(base_ref[rows, :], LANES - reach, 1, stride=1, stride_axis=0)


def near_mask(width):
    reach = (width - 1) // 2
    row = lax.broadcasted_iota(jnp.int32, (LANES, LANES), 0)
    col = lax.broadcasted_iota(jnp.int32, (LANES, LANES), 1)
    return jnp.abs(row - col) <= reach


def border_kernel(volume_ref, background_ref, psf_ref, border_ref, table_ref, volume_edge, background_edge, sems):
    frames, depth, row_count = volume_ref.shape[:3]
    half = border_ref.shape[2]
    width = volume_edge.shape[2]
    tile = lax.axis_index("tile")

    def copies(start):
        rows = pl.ds(start, width)
        return (
            pltpu.make_async_copy(volume_ref.at[:, :, rows, :], volume_edge, sems.at[0]),
            pltpu.make_async_copy(background_ref.at[:, rows, :], background_edge, sems.at[1]),
        )

    spread = pltpu.make_async_copy(psf_ref, table_ref, sems.at[2])

    @pl.when(tile == 0)
    def _():
        for copy in copies(row_count - width):
            copy.start()

    @pl.when(tile != 0)
    def _():
        for copy in copies(0):
            copy.start()

    spread.start()
    for copy in copies(0):
        copy.wait()
    for f in range(frames):
        for d in range(depth):
            total = volume_edge[f, d].astype(F32) + background_edge[d]
            border_ref[f, d] = jnp.where(tile == 0, total[width - half :], total[:half]).astype(BF16)
    spread.wait()


def forward_table_kernel(psf_ref, volume_ref, background_ref, table_ref, left_ref, edge_ref, base_ref, rows_ref, corner_ref):
    depth, taps, pitch, width = psf_ref.shape
    reach = (width - 1) // 2
    pairs = table_ref.shape[0] - 1
    fill_base(psf_ref, base_ref)
    near = near_mask(width)
    corner_ref[...] = jnp.zeros_like(corner_ref)
    for d in range(depth):
        for t in range(2 * pairs):
            pair, lanes = t // 2, pl.ds((t % 2) * LANES, LANES)
            if t < taps:
                band = rotated(base_ref, (d * taps + t) * pitch, pitch)
                table_ref[pair, pl.ds(d * LANES, LANES), lanes] = jnp.where(near, band, 0.0).astype(BF16)
                far = jnp.where(near, 0.0, band)
                half_row = LANES * (pair // 4)
                shift = d * (LANES // 2) + edge_shift(pair % 4)
                corner_ref[pl.ds(half_row + shift, reach), lanes] = far[:reach]
                corner_ref[pl.ds(half_row + (LANES - reach + shift) % LANES, reach), lanes] = far[LANES - reach :]
            else:
                table_ref[pair, pl.ds(d * LANES, LANES), lanes] = jnp.zeros((LANES, LANES), BF16)
    table_ref[pairs] = corner_ref[...].astype(BF16)
    frames, depth, row_count, col_count = volume_ref.shape
    blocks = col_count // LANES
    half = (taps - 1) // 2
    tile = lax.axis_index("tile")
    masks = edge_masks(blocks, blocks, reach)
    span = left_ref.shape[0] // frames
    for f in range(frames):
        for d in range(depth):
            base = (f * depth + d) * row_count * blocks
            for j in range(blocks):
                lanes = pl.ds(j * LANES, LANES)
                total = (volume_ref[f, d, :, lanes].astype(F32) + background_ref[d, :, lanes]).astype(BF16).astype(F32)
                rows_ref[pl.ds(PAD + base + j, row_count, stride=blocks), :] = total
        own = f * span + half * blocks
        empty = pl.ds(pl.multiple_of(f * span + (row_count + half) * blocks * tile, blocks), half * blocks)
        last = pl.ds((f + 1) * span - blocks, blocks)
        left_ref[empty, :] = jnp.zeros((half * blocks, depth * LANES), BF16)
        edge_ref[empty, :] = jnp.zeros((half * blocks, LANES), F32)
        left_ref[last, :] = jnp.zeros((blocks, depth * LANES), BF16)
        edge_ref[last, :] = jnp.zeros((blocks, LANES), F32)
        for r in range(row_count):
            starts = [PAD + ((f * depth + d) * row_count + r) * blocks for d in range(depth)]
            rows = pl.ds(own + r * blocks, blocks)
            left_ref[rows, :], edge_ref[rows, :] = joined(rows_ref, starts, blocks, masks)


def backward_table_kernel(psf_ref, measured_ref, table_ref, inverse_ref, chunk_ref, base_ref, rows_ref):
    depth, taps, pitch, width = psf_ref.shape
    frames, row_count, col_count = measured_ref.shape
    blocks = col_count // LANES
    chunk_rows = chunk_ref.shape[1]
    fill_base(psf_ref, base_ref)
    near = near_mask(width)
    for d in range(depth):
        total = jnp.zeros((1, LANES), F32)
        lanes = pl.ds(d * LANES, LANES)
        for t in range(taps):
            band = rotated(base_ref, (d * taps + t) * pitch, pitch).T
            total = total + jnp.sum(band, axis=0, keepdims=True)
            table_ref[t, pl.ds(0, LANES), lanes] = jnp.where(near, band, 0.0).astype(BF16)
            table_ref[t, pl.ds(LANES, LANES), lanes] = jnp.where(near, 0.0, band).astype(BF16)
        inverse_ref[d] = 1.0 / total
    place = lax.axis_index("depth")
    per_frame = rows_ref.shape[0] // frames
    if per_frame > row_count * blocks:
        rows_ref[...] = jnp.ones_like(rows_ref)
    for f in range(frames):
        start = f * per_frame
        for j in range(blocks):
            lanes = pl.ds(j * LANES, LANES)
            rows_ref[pl.ds(start + j, row_count, stride=blocks), :] = measured_ref[f, :, lanes].astype(F32)
        for r in range(chunk_rows):
            at = pl.multiple_of(start + (place * chunk_rows + r) * blocks, blocks)
            chunk_ref[f, r] = rows_ref[pl.ds(at, blocks), :]


def with_edges(rows_ref, start, count, blocks, after_mask, before_mask):
    here = rows_ref[pl.ds(start, count), :]
    after = rows_ref[pl.ds(start + 1, count), :]
    before = rows_ref[pl.ds(start - 1, count), :]
    edges = jnp.where(after_mask, after, jnp.where(before_mask, before, 0.0))
    return here.astype(BF16), edges


def edge_masks(count, blocks, reach=LANES // 2):
    row = lax.rem(lax.broadcasted_iota(jnp.int32, (count, LANES), 0), blocks)
    lane = lax.broadcasted_iota(jnp.int32, (count, LANES), 1)
    after = jnp.logical_and(lane < reach, row < blocks - 1)
    before = jnp.logical_and(lane >= LANES - reach, row > 0)
    return after, before


PAD = 8


def partners(chunks):
    return [0] + sorted(range(1, chunks), key=lambda mask: (mask != chunks - 1, mask))


def sensor_kernel(chunks, row_count, half, reach, given_ref, given_edge_ref, got_ref, table_ref, own_ref, *rest):
    sent_refs = rest[: chunks - 1]
    left_ref, edge_ref, rows_ref, packed_ref, sums_ref, whole_ref = rest[chunks - 1 :]
    frames, depth, halo, col_count = got_ref.shape
    blocks = col_count // LANES
    pairs = table_ref.shape[0] - 1
    sensor_rows = row_count
    span = left_ref.shape[0] // frames
    tile = lax.axis_index("tile")
    place = lax.axis_index("depth")
    masks = edge_masks(blocks, blocks, reach)
    for f in range(frames):
        for d in range(depth):
            first = (f * depth + d) * halo * blocks
            for j in range(blocks):
                lanes = pl.ds(j * LANES, LANES)
                rows_ref[pl.ds(PAD + first + j, halo, stride=blocks), :] = got_ref[f, d, :, lanes].astype(F32)
        other = f * span + (row_count + half) * blocks * (1 - tile)
        for r in range(halo):
            starts = [PAD + ((f * depth + d) * halo + r) * blocks for d in range(depth)]
            rows = pl.ds(pl.multiple_of(other + r * blocks, blocks), blocks)
            left_ref[rows, :], edge_ref[rows, :] = joined(rows_ref, starts, blocks, masks)
    size = (sensor_rows + 1) * blocks
    chunk_rows = own_ref.shape[1]
    for f in range(frames):
        for r in range(sensor_rows + 1):
            packed = None
            for pair in range(4):
                values = edge_ref[pl.ds(f * span + (r + 2 * pair) * blocks, blocks), :]
                if pair:
                    values = pltpu.roll(values, edge_shift(pair), 1)
                packed = values if packed is None else packed + values
            rows = pl.ds((f * (sensor_rows + 1) + r) * blocks, blocks)
            packed_ref[rows, pl.ds(0, LANES)] = packed.astype(BF16)
            packed_ref[rows, pl.ds(LANES, LANES)] = edge_ref[pl.ds(f * span + (r + 8) * blocks, blocks), :].astype(BF16)
    for f in range(frames):
        total = None
        for p in range(pairs + 1):
            if p < pairs:
                left = left_ref[pl.ds(f * span + 2 * p * blocks, size), :]
            else:
                left = packed_ref[pl.ds(f * size, size), :]
            product = jnp.dot(left, table_ref[p], preferred_element_type=F32)
            total = product if total is None else total + product
        sums_ref[...] = total
        count = sensor_rows * blocks
        whole_ref[f, pl.ds(0, count), :] = sums_ref[pl.ds(0, count), pl.ds(0, LANES)] + sums_ref[pl.ds(blocks, count), pl.ds(LANES, LANES)]
        if whole_ref.shape[1] > count:
            whole_ref[f, pl.ds(count, whole_ref.shape[1] - count), :] = jnp.ones((whole_ref.shape[1] - count, LANES), F32)
        for s in range(chunks):
            target = place if s == 0 else lax.bitwise_xor(place, partners(chunks)[s])
            for r in range(chunk_rows):
                start = pl.multiple_of((target * chunk_rows + r) * blocks, blocks)
                values = whole_ref[f, pl.ds(start, blocks), :]
                if s == 0:
                    own_ref[f, r] = values
                else:
                    sent_refs[s - 1][f, r] = values.astype(BF16)


def joined(rows_ref, starts, blocks, masks):
    (one, one_edges), (two, two_edges) = [with_edges(rows_ref, start, blocks, blocks, *masks) for start in starts]
    return jnp.concatenate([one, two], axis=1), one_edges + pltpu.roll(two_edges, LANES // 2, 1)


def edge_shift(pair):
    return 32 * (pair % 2) + 16 * (pair // 2)


def spread_ratio(images, row_count, half, blocks, fill, border, rows_ref, left_ref):
    tile = lax.axis_index("tile")
    masks = edge_masks(blocks, blocks)
    windows = row_count + 2 * half
    for f in range(images):
        first = PAD + f * windows * blocks
        fill(f, first + half * blocks)
        for r in range(half):
            at = first + ((row_count + half) * (1 - tile) + r) * blocks
            rows_ref[pl.ds(pl.multiple_of(at, 8), blocks), :] = border(f, r)
        empty = pl.multiple_of(first + (row_count + half) * blocks * tile, 8)
        rows_ref[pl.ds(empty, half * blocks), :] = jnp.zeros((half * blocks, LANES), F32)
        for r in range(windows):
            here, edges = with_edges(rows_ref, first + r * blocks, blocks, blocks, *masks)
            rows = pl.ds((f * windows + r) * blocks, blocks)
            left_ref[rows, pl.ds(0, LANES)] = here
            left_ref[rows, pl.ds(LANES, LANES)] = edges.astype(BF16)


def sum_kernel(*refs):
    for s, chunk_ref in enumerate(refs[:-1]):
        frames, chunk_rows = chunk_ref.shape[:2]
        for r in range(chunk_rows):
            total = chunk_ref[0, r].astype(F32)
            for f in range(1, frames):
                total = total + chunk_ref[f, r].astype(F32)
            refs[-1][s, r] = total.astype(BF16)


def collect_kernel(chunks, row_count, *refs):
    ratio_refs = refs[:chunks]
    image_ref, border_ref, border_sum_ref = refs[chunks:]
    frames, chunk_rows = ratio_refs[0].shape[:2]
    half = border_ref.shape[1]
    place = lax.axis_index("depth")
    for s, mask in enumerate(partners(chunks)):
        source = lax.bitwise_xor(place, mask) if s else place
        for r in range(chunk_rows):
            for f in range(frames):
                image_ref[f, source * chunk_rows + r] = ratio_refs[s][f, r]
    edge = (row_count - half) * (1 - lax.axis_index("tile"))
    for r in range(half):
        total = None
        for f in range(frames):
            values = image_ref[f, edge + r]
            border_ref[f, r] = values
            values = values.astype(F32)
            total = values if total is None else total + values
        border_sum_ref[r] = total.astype(BF16)


def backproject(f, span, taps, row_count, blocks, left_ref, table_ref):
    total = None
    for t in range(taps):
        left = left_ref[pl.ds(f * span + (taps - 1 - t) * blocks, row_count * blocks), :]
        product = jnp.dot(left, table_ref[t], preferred_element_type=F32)
        total = product if total is None else total + product
    return total


def volume_kernel(image_ref, border_ref, volume_ref, table_ref, inverse_ref, out_ref, rows_ref, left_ref, sums_ref):
    frames, depth, row_count, col_count = volume_ref.shape
    half = border_ref.shape[1]
    blocks = col_count // LANES
    taps = table_ref.shape[0]

    def fill(f, start):
        for r in range(row_count):
            rows_ref[pl.ds(start + r * blocks, blocks), :] = image_ref[f, r].astype(F32)

    spread_ratio(
        frames,
        row_count,
        half,
        blocks,
        fill,
        lambda f, r: border_ref[f, r].astype(F32),
        rows_ref,
        left_ref,
    )
    span = (row_count + 2 * half) * blocks
    for f in range(frames):
        total = backproject(f, span, taps, row_count, blocks, left_ref, table_ref)
        for d in range(depth):
            start = (f * depth + d) * row_count * blocks
            sums_ref[pl.ds(start, row_count * blocks), :] = total[:, d * LANES : (d + 1) * LANES]
            for j in range(blocks):
                lanes = pl.ds(j * LANES, LANES)
                back = sums_ref[pl.ds(start + j, row_count, stride=blocks), :]
                value = volume_ref[f, d, :, lanes].astype(F32) * back * inverse_ref[d]
                out_ref[f, d, :, lanes] = value.astype(BF16)


def background_kernel(chunks, scale, late_ref, early_ref, late_got_ref, early_got_ref, border_ref, border_got_ref, background_ref, table_ref, inverse_ref, given_ref, out_ref, given_out_ref, rows_ref, left_ref, sums_ref, stage_ref, sems):
    given = pltpu.make_async_copy(given_ref, given_out_ref, sems.at[0])
    given.start()
    depth, row_count, col_count = background_ref.shape
    half = border_ref.shape[0]
    blocks = col_count // LANES
    taps = table_ref.shape[0]
    place = lax.axis_index("depth")
    early, chunk_rows = early_ref.shape[:2]

    def fill(f, start):
        for s, mask in enumerate(partners(chunks)):
            source = lax.bitwise_xor(place, mask) if s else place
            own, got, slot = (early_ref, early_got_ref, s) if s < early else (late_ref, late_got_ref, s - early)
            for r in range(chunk_rows):
                at = pl.multiple_of(start + (source * chunk_rows + r) * blocks, 8)
                rows_ref[pl.ds(at, blocks), :] = own[slot, r].astype(F32) + got[slot, r].astype(F32)

    spread_ratio(
        1,
        row_count,
        half,
        blocks,
        fill,
        lambda f, r: border_ref[r].astype(F32) + border_got_ref[r].astype(F32),
        rows_ref,
        left_ref,
    )
    span = (row_count + 2 * half) * blocks
    total = backproject(0, span, taps, row_count, blocks, left_ref, table_ref)
    copies = [given]
    for d in range(depth):
        start = d * row_count * blocks
        sums_ref[pl.ds(start, row_count * blocks), :] = total[:, d * LANES : (d + 1) * LANES]
        for j in range(blocks):
            lanes = pl.ds(j * LANES, LANES)
            back = sums_ref[pl.ds(start + j, row_count, stride=blocks), :]
            stage_ref[d, :, lanes] = background_ref[d, :, lanes] * back * (inverse_ref[d] * scale)
        copies.append(pltpu.make_async_copy(stage_ref.at[d], out_ref.at[d], sems.at[1 + d]))
        copies[-1].start()
    for copy in copies:
        copy.wait()


def whole(count):
    return [pl.BlockSpec(memory_space=pltpu.VMEM)] * count


def call(kernel, args, outs, scratch, flops, aliases={}, place=pltpu.VMEM):
    moved = sum(a.size * a.dtype.itemsize for a in args)
    return pl.pallas_call(
        kernel,
        out_shape=outs,
        in_specs=whole(len(args)),
        out_specs=jax.tree.map(lambda _: pl.BlockSpec(memory_space=place), outs),
        scratch_shapes=scratch,
        input_output_aliases=aliases,
        compiler_params=pltpu.CompilerParams(vmem_limit_bytes=40 * 2**20),
        cost_estimate=pl.CostEstimate(flops=flops, bytes_accessed=min(moved, flops // 100), transcendentals=0),
    )(*args)


def body(volume, background, measured, psf):
    frames, depth, row_count, col_count = volume.shape
    taps, pitch, width = psf.shape[1:]
    half = (taps - 1) // 2
    reach = (width - 1) // 2
    blocks = col_count // LANES
    pairs = (taps + 1) // 2
    chunks = lax.axis_size("depth")
    splits = lax.axis_size("tm")
    chunk_rows = -(-row_count // chunks)
    padded_rows = chunks * chunk_rows
    windows = row_count + 2 * half
    shape = jax.ShapeDtypeStruct
    vmem = pltpu.VMEM

    swap = [(0, 1), (1, 0)]
    edge_rows = 8 * -(-half // 8)
    sent, table = pl.pallas_call(
        border_kernel,
        out_shape=(shape((frames, depth, half, col_count), BF16), shape(psf.shape, BF16)),
        in_specs=[pl.BlockSpec(memory_space=pltpu.HBM)] * 3,
        out_specs=(pl.BlockSpec(memory_space=pltpu.VMEM),) * 2,
        scratch_shapes=[
            vmem((frames, depth, edge_rows, col_count), BF16),
            vmem((depth, edge_rows, col_count), F32),
            pltpu.SemaphoreType.DMA((3,)),
        ],
        compiler_params=pltpu.CompilerParams(vmem_limit_bytes=8 * 2**20),
    )(*[pltpu.with_memory_space_constraint(a, pltpu.HBM) for a in (volume, background, psf)])
    border = lax.ppermute(sent, "tile", swap)

    base = vmem((depth * taps * pitch, LANES), F32)
    assert depth == 2 and pairs == 5 and 16 * reach == LANES
    left_shape = shape((frames * (windows + 1) * blocks, depth * LANES), BF16)
    edge_shape = shape((frames * (windows + 1) * blocks, LANES), F32)
    forward, left, left_edge = call(
        forward_table_kernel,
        (table, volume, background),
        (shape((pairs + 1, 2 * LANES, 2 * LANES), BF16), left_shape, edge_shape),
        [base, vmem((frames * depth * row_count * blocks + 2 * PAD, LANES), F32), vmem((2 * LANES, 2 * LANES), F32)],
        2 * 10**8,
    )
    chunk = (frames, chunk_rows, blocks, LANES)
    parts = call(
        functools.partial(sensor_kernel, chunks, row_count, half, reach),
        (left, left_edge, border, forward),
        (shape(chunk, F32),) + (shape(chunk, BF16),) * (chunks - 1) + (left_shape, edge_shape),
        [
            vmem((frames * depth * half * blocks + 2 * PAD, LANES), F32),
            vmem((frames * (row_count + 1) * blocks, 2 * LANES), BF16),
            vmem(((row_count + 1) * blocks, 2 * LANES), F32),
            vmem((frames, padded_rows * blocks, LANES), F32),
        ],
        2 * 10**9,
        {0: chunks, 1: chunks + 1},
    )
    sensor = parts[0]
    masks = partners(chunks)
    moved = [
        lax.ppermute(parts[s], "depth", [(i, i ^ masks[s]) for i in range(chunks)])
        for s in range(1, chunks)
    ]
    backward, inverse, measured_chunk = call(
        backward_table_kernel,
        (table, measured),
        (
            shape((taps, 2 * LANES, depth * LANES), BF16),
            shape((depth, 1, LANES), F32),
            shape(chunk, F32),
        ),
        [base, vmem((frames * padded_rows * blocks, LANES), F32)],
        2 * 10**8,
    )
    for part in moved:
        sensor = sensor + part.astype(F32)
    ratio = (measured_chunk / sensor).astype(BF16)
    ratios = [ratio] + [
        lax.ppermute(ratio, "depth", [(i, i ^ masks[s]) for i in range(chunks)])
        for s in range(1, chunks)
    ]
    early = max(1, chunks // 2)
    pieces = [
        call(sum_kernel, tuple(part), shape((len(part),) + chunk[1:], BF16), [], 10**6)
        for part in (ratios[:early], ratios[early:])
    ]
    image, edge, edge_sum = call(
        functools.partial(collect_kernel, chunks, row_count),
        tuple(ratios),
        (
            shape((frames, padded_rows, blocks, LANES), BF16),
            shape((frames, half, blocks, LANES), BF16),
            shape((half, blocks, LANES), BF16),
        ),
        [],
        10**9,
    )
    if splits == 2:
        got = [lax.ppermute(piece, "tm", swap) for piece in pieces]
        other_got = lax.ppermute(edge_sum, ("tm", "tile"), [(i, 3 - i) for i in range(4)])
    edge = lax.ppermute(edge, "tile", swap)
    other = jnp.sum(edge.astype(F32), axis=0)
    if splits == 2:
        other = other.astype(BF16)
    else:
        pieces = [lax.psum(piece.astype(F32), "tm").astype(BF16) for piece in pieces]
        other = lax.psum(other.astype(BF16).astype(F32), "tm").astype(BF16)
        got, other_got = [jnp.zeros_like(piece) for piece in pieces], jnp.zeros_like(other)
    new_volume = call(
        volume_kernel,
        (image, edge, volume, backward, inverse),
        shape(volume.shape, BF16),
        [
            vmem((frames * windows * blocks + 2 * PAD, LANES), F32),
            vmem((frames * windows * blocks, 2 * LANES), BF16),
            vmem((frames * depth * row_count * blocks, LANES), F32),
        ],
        100000000,
    )
    new_background, new_volume = call(
        functools.partial(background_kernel, chunks, 1.0 / (frames * splits)),
        (*pieces[::-1], *got[::-1], other, other_got, background, backward, inverse, new_volume),
        (shape(background.shape, F32), shape(volume.shape, BF16)),
        [
            vmem((windows * blocks + 2 * PAD, LANES), F32),
            vmem((windows * blocks, 2 * LANES), BF16),
            vmem((depth * row_count * blocks, LANES), F32),
            vmem(background.shape, F32),
            pltpu.SemaphoreType.DMA((1 + depth,)),
        ],
        10**9,
        place=pl.ANY,
    )
    return new_volume, new_background


def solution(mesh):
    placed = (
        P(("groups", "tm"), "depth", "tile", None),
        P(("groups", "depth"), "tile", None),
        P(("groups", "tm"), "tile", None),
        P("depth", None, None, None),
    )
    return jax.shard_map(
        body,
        mesh=mesh,
        in_specs=placed,
        out_specs=(
            P(("groups", "tm"), "depth", "tile", None),
            P(("groups", "depth"), "tile", None),
        ),
        check_vma=False,
    )
```
